32 devices in a mesh: gx: 4 (over z), gy: 8 (over y, x, core).
Axes of the slice: x: 2, y: 2, z: 4, core: 2. Of those that a mesh axis runs over, the one named last changes fastest.
Arguments:
- snapshots: float32 [28, 64, 6144], P(None, 'gx', 'gy'), may hold values from -16 to 16
- modes: float32 [64, 64, 6144], P(None, 'gx', 'gy'), may hold values from -8 to 8
- mobility: float32 [64, 6144], P('gx', 'gy'), may hold values from 0.03 to 0.16
- phase: int32 [64, 6144], P('gx', 'gy'), may hold values 0 or 1
- contact: int32 [64, 6144], P('gx', 'gy'), may hold values 0 or 1
- sigma: float32 [64], replicated, may hold values from 1 to 10
Outputs:
- basis: float32 [28, 64, 6144], P(None, 'gx', 'gy')
- core: float32 [92, 92], replicated
The draws below stay inside these ranges and needn't reach their ends.
All inputs are finite; a program needn't handle non-finite values. No bound on the sum of `phase` or of `contact` on one device may be relied on, other than what follows from the above.
Results may differ from the reference program's by a relative error of at most 0.00028.
Values sent between devices are 32-bit elements; how exact they have to be, the bound alone decides.
No kernel may reach another device: no remote copies, remote signals or barrier semaphores. Data moves between devices by JAX's collectives and lax.ppermute only.
A program may use at most 192 MiB of HBM per device.

```python
import math
import jax
import jax.numpy as jnp
from jax import lax

NZ = 24
K = 64
B = 28
STEPS = 3
NX = 64
NY = 256
NYZ = 6144


def mode_fields(key, count):
    keys = jax.random.split(jax.random.fold_in(key, 11), K)[:count]

    def single(one_key):
        return jnp.clip(jax.random.normal(one_key, (NX, NY * NZ), jnp.float32), -6.0, 6.0)
    return jax.vmap(single)(keys)


def draw_modes(key, part):
    return mode_fields(key, K)


def draw_snapshots(key, part):
    paired = mode_fields(key, B)
    base = jnp.clip(jax.random.normal(jax.random.fold_in(key, 21), (NX, NY * NZ), jnp.float32), -6.0, 6.0)
    noise = jnp.clip(jax.random.normal(jax.random.fold_in(key, 22), (B, NX, NY * NZ), jnp.float32), -6.0, 6.0)
    return base[None] + 0.8 * paired + 0.6 * noise


def with_ends(entries, own_key, smallest, largest):
    dims = entries.shape
    place = [jax.random.randint(jax.random.fold_in(own_key, axis), (), 0, dims[axis]) for axis in range(len(dims))]
    entries = entries.at[tuple(place)].set(smallest)
    longest = dims.index(max(dims))
    place[longest] = (place[longest] + 1) % dims[longest]
    return entries.at[tuple(place)].set(largest)


def steps_of(own_key, shape, cuts, smallest, largest):
    gain, own = 1.0, jax.random.fold_in(own_key, 6)
    for dim, shards_of in cuts:
        draws = jnp.exp(jax.random.uniform(jax.random.fold_in(own, dim), (shards_of,), jnp.float32, smallest / len(cuts), largest / len(cuts)))
        gain = gain * jnp.repeat(draws, shape[dim] // shards_of).reshape([-1 if axis == dim else 1 for axis in range(len(shape))])
    return gain


def setup_inputs(seed: int = 0) -> dict:
    splits = jax.random.split(jax.random.key(seed), 7)
    return {
        "snapshots": draw_snapshots(jax.random.fold_in(splits[6], 71), 0),
        "modes": draw_modes(jax.random.fold_in(splits[6], 71), 0),
        "mobility": jnp.clip(jnp.exp(math.log(0.16) - 1.6739764 * jax.random.uniform(splits[2], (NX, NYZ), jnp.float32) ** steps_of(splits[2], (NX, NYZ), ((0, 4), (1, 8)), -0.2, 0.2)), 0.03, 0.16),
        "phase": with_ends((jax.random.randint(splits[3], (NX, NYZ), 0, 2) < 1).astype(jnp.int32), jax.random.fold_in(splits[3], 1), 0, 1),
        "contact": with_ends((jax.random.randint(splits[4], (NX, NYZ), 0, 8) < 1).astype(jnp.int32), jax.random.fold_in(splits[4], 1), 0, 1),
        "sigma": jnp.clip(jnp.exp(jax.random.uniform(splits[5], (K,), jnp.float32, math.log(1.0), math.log(10.0))), 1.0, 10.0),
    }


def advance(field, rate, pin):
    ext = jnp.pad(field, ((0, 0), (1, 1), (1, 1), (0, 0)))
    below = jnp.concatenate([field[:, :, :, :1], field[:, :, :, :-1]], axis=3)
    above = jnp.concatenate([field[:, :, :, 1:], field[:, :, :, -1:]], axis=3)
    beside = ext[:, 2:, 1:-1] + ext[:, :-2, 1:-1] + ext[:, 1:-1, 2:] + ext[:, 1:-1, :-2] + below + above
    return field + rate * (beside - 6.0 * field) - pin * field

def reference(snapshots, modes, mobility, phase, contact, sigma):
    highest = lax.Precision.HIGHEST
    rate = mobility * jnp.where(phase == 1, 1.0, 0.5).astype(jnp.float32)
    pin = 0.25 * contact.astype(jnp.float32)
    rate = rate.reshape(NX, NY, NZ)
    pin = pin.reshape(NX, NY, NZ)
    field = snapshots.reshape(B, NX, NY, NZ)
    for step in range(STEPS):
        field = advance(field, rate, pin)
    ncell = float(NX * NY * NZ)
    flat_modes = modes.reshape(K, -1)
    flat = field.reshape(B, -1)
    first = jnp.dot(flat_modes, flat.T, precision=highest) / ncell
    partial_value = flat - jnp.dot(first.T, flat_modes, precision=highest)
    second = jnp.dot(flat_modes, partial_value.T, precision=highest) / ncell
    remain = partial_value - jnp.dot(second.T, flat_modes, precision=highest)
    gram = jnp.dot(remain, remain.T, precision=highest) / ncell
    lower = jnp.linalg.cholesky(gram)
    basis = jax.scipy.linalg.solve_triangular(lower, remain, lower=True).reshape(snapshots.shape)
    upper_rows = jnp.concatenate([jnp.diag(sigma), first + second], axis=1)
    lower_rows = jnp.concatenate([jnp.zeros((B, K), jnp.float32), lower.T], axis=1)
    core = jnp.concatenate([upper_rows, lower_rows], axis=0)
    return (basis, core)
```

```python
import jax
import jax.numpy as jnp
from jax import lax
from jax.experimental import pallas as pl
from jax.experimental.pallas import tpu as pltpu
from jax.sharding import PartitionSpec as P

NZ = 24
STEPS = 3
LANES = 128
ROWS = 32
HIGH = lax.Precision.HIGHEST
F32 = jnp.float32
BF16 = jnp.bfloat16


def split(value):
    high = value.astype(BF16)
    return high, (value - high.astype(F32)).astype(BF16)


def dot_t(a, b):
    return lax.dot_general(a, b, (((1,), (1,)), ((), ())), preferred_element_type=F32)


def small_dot(a, b, dims=((1,), (0,))):
    return lax.dot_general(a, b, (dims, ((), ())), precision=HIGH, preferred_element_type=F32)


def prep_kernel(snap, mob, pha, con, f0, sxa, sxb, sya, syb, buf, sem):
    batch, cols, width = snap.shape
    copies = [pltpu.make_async_copy(snap.at[:, i, :], buf.at[i], sem.at[i]) for i in range(cols)]
    for copy in copies:
        copy.start()
    rate = mob[...] * jnp.where(pha[...] == 1, 1.0, 0.5).astype(F32)
    lane = lax.broadcasted_iota(jnp.int32, (cols, width), 1) % NZ
    ends = jnp.where(lane == 0, 1.0, 0.0) + jnp.where(lane == NZ - 1, 1.0, 0.0)
    keep = 1.0 - 0.25 * con[...].astype(F32) - rate * (6.0 - ends)
    for i in range(cols):
        copies[i].wait()
        f0[i, 0:batch, :] = buf[i]
        f0[i, batch : batch + 1, :] = rate[i : i + 1, :]
        f0[i, batch + 1 : batch + 2, :] = keep[i : i + 1, :]
        f0[i, batch + 2 : ROWS, :] = jnp.zeros((ROWS - batch - 2, width), F32)
    odd_x = lax.rem(lax.axis_index("gx"), 2)
    odd_y = lax.rem(lax.axis_index("gy"), 2)
    far = cols - STEPS
    sxa[...] = f0[pl.ds((1 - odd_x) * far, STEPS)]
    sxb[...] = f0[pl.ds(odd_x * far, STEPS)]
    edge = width // LANES - 1
    sya[...] = f0[:, :, pl.ds(pl.multiple_of((1 - odd_y) * edge * LANES, LANES), LANES)]
    syb[...] = f0[:, :, pl.ds(pl.multiple_of(odd_y * edge * LANES, LANES), LANES)]


def modes_kernel(modes, ub, gram, buf, acc, sem):
    count, cols, width = modes.shape
    copies = [pltpu.make_async_copy(modes.at[:, i, :], buf.at[i], sem.at[i]) for i in range(cols)]
    for copy in copies:
        copy.start()
    for i in range(cols):
        copies[i].wait()
        high, low = split(buf[i])
        ub[i, 0:count, :] = high
        ub[i, count : 2 * count, :] = low
        both = ub[i]
        part = dot_t(both, both)
        acc[...] = part if i == 0 else acc[...] + part
    gram[...] = (acc[0:count, 0:count] + acc[count : 2 * count, count : 2 * count]) + (
        acc[0:count, count : 2 * count] + acc[count : 2 * count, 0:count]
    )


def step_row(src, base, row, group, batch):
    s = pl.ds(group * 8, 8)
    here = src[row, s, :]
    width = here.shape[1]
    lane = lax.broadcasted_iota(jnp.int32, here.shape, 1)
    z = (lane + 16) % NZ
    below = jnp.where(z == 0, 0.0, pltpu.roll(here, 1, 1))
    above = jnp.where(z == NZ - 1, 0.0, pltpu.roll(here, width - 1, 1))
    beside = (src[row - 1, s, :] + src[row + 1, s, :]) + (
        pltpu.roll(here, NZ, 1) + pltpu.roll(here, width - NZ, 1)
    )
    rate = base[row, batch : batch + 1, :]
    keep = base[row, batch + 1 : batch + 2, :]
    return keep * here + rate * (beside + (below + above))


def step_kernel(batch, f0, hxa, hxb, hya, hyb, ca, cb, ub, s_gram, x3b, out, e0, e1, e2, acc_u, acc_x):
    cols = f0.shape[0]
    width = f0.shape[2]
    left, right = LANES, LANES + width
    odd_x = lax.rem(lax.axis_index("gx"), 2) == 1
    odd_y = lax.rem(lax.axis_index("gy"), 2) == 1
    e0[0:STEPS, :, 0:left] = jnp.zeros((STEPS, ROWS, LANES), F32)
    e0[0:STEPS, :, right:] = jnp.zeros((STEPS, ROWS, LANES), F32)
    e0[cols + STEPS :, :, 0:left] = jnp.zeros((STEPS, ROWS, LANES), F32)
    e0[cols + STEPS :, :, right:] = jnp.zeros((STEPS, ROWS, LANES), F32)
    e0[STEPS : cols + STEPS, :, left:right] = f0[...]

    def place_x(up, down):
        e0[0:STEPS, :, left:right] = up[...]
        e0[cols + STEPS :, :, left:right] = down[...]

    def place_y(low, high, corner_low, corner_high):
        e0[STEPS : cols + STEPS, :, 0:left] = low[...]
        e0[STEPS : cols + STEPS, :, right:] = high[...]
        e0[1:STEPS, :, 0:left] = corner_low[0:2]
        e0[1:STEPS, :, right:] = corner_high[0:2]
        e0[cols + STEPS : cols + STEPS + 2, :, 0:left] = corner_low[2:4]
        e0[cols + STEPS : cols + STEPS + 2, :, right:] = corner_high[2:4]

    pl.when(odd_x)(lambda: place_x(hxa, hxb))
    pl.when(jnp.logical_not(odd_x))(lambda: place_x(hxb, hxa))
    pl.when(odd_y)(lambda: place_y(hya, hyb, ca, cb))
    pl.when(jnp.logical_not(odd_y))(lambda: place_y(hyb, hya, cb, ca))

    @pl.loop(1, cols + 5)
    def _(row):
        for group in range(4):
            e1[row, pl.ds(group * 8, 8), :] = step_row(e0, e0, row, group, batch)

    @pl.loop(2, cols + 4)
    def _(row):
        for group in range(4):
            e2[row, pl.ds(group * 8, 8), :] = step_row(e1, e0, row, group, batch)

    acc_u[...] = jnp.zeros_like(acc_u)
    acc_x[...] = jnp.zeros_like(acc_x)

    @pl.loop(0, cols)
    def _(i):
        for group in range(2):
            new = jnp.concatenate(
                [step_row(e2, e0, i + STEPS, 2 * group + k, batch)[:, left:right] for k in range(2)], 0
            )
            high, low = split(new)
            x3b[i, pl.ds(group * 16, 16), :] = high
            x3b[i, pl.ds(ROWS + group * 16, 16), :] = low
        both = x3b[i]
        acc_u[...] += dot_t(ub[i], both)
        acc_x[...] += dot_t(both, both)

    count = ub.shape[1] // 2
    u = acc_u[0:count, :] + acc_u[count:, :]
    x = acc_x[0:ROWS, :] + acc_x[ROWS:, :]
    out[...] = jnp.zeros_like(out)
    out[:, 0:ROWS] = u[:, 0:ROWS] + u[:, ROWS:]
    out[0:ROWS, ROWS : 2 * ROWS] = x[:, 0:ROWS] + x[:, ROWS:]
    out[:, 2 * ROWS :] = s_gram[...]


def last_kernel(batch, cells, total, sigma, x3b, ub, basis, core, buf, sem):
    cols = x3b.shape[0]
    count = ub.shape[1] // 2
    inverse = 1.0 / cells
    col = lax.broadcasted_iota(jnp.int32, (count, ROWS), 1)
    c = jnp.where(col < batch, total[:, 0:ROWS], 0.0)
    rows = lax.broadcasted_iota(jnp.int32, (ROWS, ROWS), 0)
    lanes = lax.broadcasted_iota(jnp.int32, (ROWS, ROWS), 1)
    g = total[0:ROWS, ROWS : 2 * ROWS]
    s = total[:, 2 * ROWS :]
    first = c * inverse
    both = first + (c - small_dot(s, first)) * inverse
    rest = small_dot(s, both) - c
    gram = g - small_dot(c, both, ((0,), (0,))) + small_dot(both, rest, ((0,), (0,)))
    gram = jnp.where((rows < batch) & (lanes < batch), gram * inverse, jnp.where(rows == lanes, 1.0, 0.0))
    m = jnp.concatenate([gram, jnp.where(rows == lanes, 1.0, 0.0)], 1)
    wide = lax.broadcasted_iota(jnp.int32, (ROWS, 2 * ROWS), 0)
    scale = jnp.ones((ROWS, 1), F32)
    for j in range(batch):
        pivot = m[j : j + 1, :]
        d = pivot[:, j : j + 1]
        scale = jnp.where(wide[:, 0:1] == j, d, scale)
        factor = jnp.where(wide > j, m[:, j : j + 1] / d, 0.0)
        m = m - factor * pivot
    m = m * lax.rsqrt(scale)
    upper = jnp.where(rows <= lanes, m[:, 0:ROWS], 0.0)
    linv = m[:, ROWS:]
    wu = -small_dot(linv, both, ((1,), (1,)))
    core[...] = jnp.zeros_like(core)
    er = lax.broadcasted_iota(jnp.int32, (count, count), 0)
    ec = lax.broadcasted_iota(jnp.int32, (count, count), 1)
    core[0:count, 0:count] = jnp.where(er == ec, sigma[...], 0.0)
    core[0:count, count:] = both[:, 0:batch]
    core[count:, count:] = upper[0:batch, 0:batch]
    xh, xl = split(linv)
    uh, ul = split(wu)
    wx = jnp.concatenate([jnp.concatenate([xh, xh], 1), jnp.concatenate([xl, xl], 1)], 0)
    wm = jnp.concatenate([jnp.concatenate([uh, uh], 1), jnp.concatenate([ul, ul], 1)], 0)
    copies = []
    for i in range(cols):
        value = jnp.dot(wx, x3b[i], preferred_element_type=F32) + jnp.dot(wm, ub[i], preferred_element_type=F32)
        buf[i] = value[0:batch] + value[ROWS : ROWS + batch]
        copy = pltpu.make_async_copy(buf.at[i], basis.at[:, i, :], sem.at[i])
        copy.start()
        copies.append(copy)
    for copy in copies:
        copy.wait()


def swap(value, axis, offset):
    count = lax.axis_size(axis)
    pairs = [(i, i + 1) for i in range(offset, count - 1, 2)]
    return lax.ppermute(value, axis, pairs + [(j, i) for i, j in pairs])


def butterfly(value):
    for axis in ("gy", "gx"):
        count = lax.axis_size(axis)
        if count & (count - 1):
            value = lax.psum(value, axis)
            continue
        step = 1
        while step < count:
            value = value + lax.ppermute(value, axis, [(i, i ^ step) for i in range(count)])
            step *= 2
    return value


def body(snapshots, modes, mobility, phase, contact, sigma):
    batch, cols, width = snapshots.shape
    count = modes.shape[0]
    vmem = pl.BlockSpec(memory_space=pltpu.VMEM)
    hbm = pl.BlockSpec(memory_space=pl.ANY)
    shape = jax.ShapeDtypeStruct
    params = pltpu.CompilerParams(vmem_limit_bytes=40 << 20)
    f0, sxa, sxb, sya, syb = pl.pallas_call(
        prep_kernel,
        out_shape=(
            shape((cols, ROWS, width), F32),
            shape((STEPS, ROWS, width), F32),
            shape((STEPS, ROWS, width), F32),
            shape((cols, ROWS, LANES), F32),
            shape((cols, ROWS, LANES), F32),
        ),
        in_specs=[hbm, vmem, vmem, vmem],
        out_specs=(vmem,) * 5,
        scratch_shapes=[pltpu.VMEM((cols, batch, width), F32), pltpu.SemaphoreType.DMA((cols,))],
        compiler_params=params,
        name="prep",
    )(snapshots, mobility, phase, contact)
    hxa = swap(sxa, "gx", 0)
    hxb = swap(sxb, "gx", 1)
    hya = swap(sya, "gy", 0)
    hyb = swap(syb, "gy", 1)
    ub, s_gram = pl.pallas_call(
        modes_kernel,
        out_shape=(shape((cols, 2 * count, width), BF16), shape((count, count), F32)),
        in_specs=[hbm],
        out_specs=(vmem, vmem),
        scratch_shapes=[
            pltpu.VMEM((cols, count, width), F32),
            pltpu.VMEM((2 * count, 2 * count), F32),
            pltpu.SemaphoreType.DMA((cols,)),
        ],
        compiler_params=params,
        cost_estimate=pl.CostEstimate(flops=2 * cols * width * 4 * count * count, bytes_accessed=8 * cols * width * count, transcendentals=0),
        name="modes",
    )(modes)
    odd_x = lax.axis_index("gx") % 2
    odd_y = lax.axis_index("gy") % 2
    up = jnp.where(odd_x == 1, hxa[1:], hxb[1:])
    down = jnp.where(odd_x == 1, hxb[:2], hxa[:2])
    ends = jnp.concatenate([up, down], 0)
    low_edge, high_edge = ends[:, :, :LANES], ends[:, :, width - LANES :]
    ca = swap(jnp.where(odd_y == 1, low_edge, high_edge), "gy", 0)
    cb = swap(jnp.where(odd_y == 1, high_edge, low_edge), "gy", 1)
    ext = (cols + 2 * STEPS, ROWS, width + 2 * LANES)
    x3b, part = pl.pallas_call(
        lambda *refs: step_kernel(batch, *refs),
        out_shape=(shape((cols, 2 * ROWS, width), BF16), shape((count, LANES), F32)),
        in_specs=[vmem] * 9,
        out_specs=(vmem, vmem),
        scratch_shapes=[
            pltpu.VMEM(ext, F32),
            pltpu.VMEM(ext, F32),
            pltpu.VMEM(ext, F32),
            pltpu.VMEM((2 * count, 2 * ROWS), F32),
            pltpu.VMEM((2 * ROWS, 2 * ROWS), F32),
        ],
        compiler_params=params,
        name="steps",
    )(f0, hxa, hxb, hya, hyb, ca, cb, ub, s_gram)
    total = butterfly(part)
    cells = float(cols * width * lax.axis_size("gx") * lax.axis_size("gy"))
    basis, core = pl.pallas_call(
        lambda *refs: last_kernel(batch, cells, *refs),
        out_shape=(shape(snapshots.shape, F32), shape((count + batch, count + batch), F32)),
        in_specs=[vmem] * 4,
        out_specs=(hbm, vmem),
        scratch_shapes=[pltpu.VMEM((cols, batch, width), F32), pltpu.SemaphoreType.DMA((cols,))],
        compiler_params=params,
        name="last",
    )(total, sigma.reshape(1, count), x3b, ub)
    return (basis, core)


def solution(mesh):
    return jax.shard_map(
        body,
        mesh=mesh,
        in_specs=(
            P(None, "gx", "gy"),
            P(None, "gx", "gy"),
            P("gx", "gy"),
            P("gx", "gy"),
            P("gx", "gy"),
            P(),
        ),
        out_specs=(P(None, "gx", "gy"), P()),
        check_vma=False,
    )
```

```python
import jax
import jax.numpy as jnp
from jax import lax
from jax.experimental import pallas as pl
from jax.experimental.pallas import tpu as pltpu
from jax.sharding import PartitionSpec as P

NZ = 24
STEPS = 3
LANES = 128
ROWS = 32
HIGH = lax.Precision.HIGHEST
F32 = jnp.float32
BF16 = jnp.bfloat16


def split(value):
    high = value.astype(BF16)
    return high, (value - high.astype(F32)).astype(BF16)


def dot_t(a, b):
    return lax.dot_general(a, b, (((1,), (1,)), ((), ())), preferred_element_type=F32)


def small_dot(a, b, dims=((1,), (0,))):
    return lax.dot_general(a, b, (dims, ((), ())), precision=HIGH, preferred_element_type=F32)


def fill_rows(dst, index, fields, rate, keep):
    batch = fields.shape[0]
    dst[index + (pl.ds(0, batch),)] = fields
    dst[index + (pl.ds(batch, 1),)] = rate
    dst[index + (pl.ds(batch + 1, 1),)] = keep
    dst[index + (pl.ds(batch + 2, ROWS - batch - 2),)] = jnp.zeros((ROWS - batch - 2, LANES), F32)


def edge_kernel(snap, mob, pha, con, coef, zsa, zsb, sxa, sxb, sya, syb, bufx, bufy, vm, vp, vc, rows, cols_y, sem, sem_c):
    batch, cols, width = snap.shape
    tiles = width // LANES
    small = [
        pltpu.make_async_copy(ref, dst, sem_c.at[i])
        for i, (ref, dst) in enumerate(((mob, vm), (pha, vp), (con, vc)))
    ]
    outer = list(range(STEPS)) + list(range(cols - STEPS, cols))
    inner = list(range(STEPS, cols - STEPS))
    copies = [pltpu.make_async_copy(snap.at[:, i, :], bufx.at[k], sem.at[k]) for k, i in enumerate(outer)]
    for k, i in enumerate(inner):
        for side, start in enumerate((0, width - LANES)):
            n = len(outer) + 2 * k + side
            copies.append(
                pltpu.make_async_copy(snap.at[:, i, pl.ds(start, LANES)], bufy.at[k, side], sem.at[n])
            )
    for copy in small + copies:
        copy.start()
    for copy in small:
        copy.wait()
    rate = vm[...] * jnp.where(vp[...] == 1, 1.0, 0.5).astype(F32)
    lane = lax.broadcasted_iota(jnp.int32, (cols, width), 1) % NZ
    ends = jnp.where(lane == 0, 1.0, 0.0) + jnp.where(lane == NZ - 1, 1.0, 0.0)
    keep = 1.0 - 0.25 * vc[...].astype(F32) - rate * (6.0 - ends)
    coef[0] = rate
    coef[1] = keep
    for k, i in enumerate(outer):
        copies[k].wait()
        for t in range(tiles):
            span = slice(t * LANES, (t + 1) * LANES)
            fill_rows(rows, (k, t), bufx[k, :, span], rate[i : i + 1, span], keep[i : i + 1, span])
        for side, t in enumerate((0, tiles - 1)):
            cols_y[side, i] = rows[k, t]
    for k, i in enumerate(inner):
        for side, t in enumerate((0, tiles - 1)):
            copies[len(outer) + 2 * k + side].wait()
            span = slice(t * LANES, (t + 1) * LANES)
            fill_rows(cols_y, (side, i), bufy[k, side], rate[i : i + 1, span], keep[i : i + 1, span])
    odd_x = lax.rem(lax.axis_index("gx"), 2)
    odd_y = lax.rem(lax.axis_index("gy"), 2)
    sxa[...] = rows[pl.ds((1 - odd_x) * STEPS, STEPS)]
    sxb[...] = rows[pl.ds(odd_x * STEPS, STEPS)]
    for row in range(2):
        for side, t in enumerate((0, tiles - 1)):
            zsa[row, side] = rows[(1 - odd_x) * (STEPS + 1) + row, t]
            zsb[row, side] = rows[odd_x * (STEPS + 1) + row, t]
    sya[...] = cols_y[1 - odd_y]
    syb[...] = cols_y[odd_y]


def modes_kernel(modes, snap, coef, ub, gram, e0, buf, bufx, acc, sem):
    count, cols, width = modes.shape
    batch = snap.shape[0]
    copies = [pltpu.make_async_copy(snap.at[:, i, :], bufx.at[i], sem.at[i]) for i in range(cols)]
    copies += [pltpu.make_async_copy(modes.at[:, i, :], buf.at[i], sem.at[cols + i]) for i in range(cols)]
    for copy in copies:
        copy.start()
    for i in range(cols):
        copies[i].wait()
        for t in range(width // LANES):
            span = slice(t * LANES, (t + 1) * LANES)
            fill_rows(e0, (i + STEPS, t), bufx[i, :, span], coef[0, i : i + 1, span], coef[1, i : i + 1, span])
    for i in range(cols):
        copies[cols + i].wait()
        high, low = split(buf[i])
        ub[i, 0:count, :] = high
        ub[i, count : 2 * count, :] = low
        both = ub[i]
        part = dot_t(both, both)
        acc[...] = part if i == 0 else acc[...] + part
    gram[...] = (acc[0:count, 0:count] + acc[count : 2 * count, count : 2 * count]) + (
        acc[0:count, count : 2 * count] + acc[count : 2 * count, 0:count]
    )


def z_masks(tiles):
    lane = lax.broadcasted_iota(jnp.int32, (8, LANES), 1)
    found = []
    for t in range(tiles + 1):
        z = (lane + t * LANES) % NZ if t < tiles else jnp.where(lane < LANES // 2, lane % NZ, (lane + 16) % NZ)
        found.append((jnp.where(z == 0, 0.0, 1.0), jnp.where(z == NZ - 1, 0.0, 1.0)))
    return found


def row_coef(base, row, batch, tiles):
    return [
        [jnp.broadcast_to(base[row, t, pl.ds(batch + k, 1), :], (8, LANES)) for k in range(2)] for t in range(tiles)
    ]


def step_row(src, coef, row, group, masks, ring, last):
    tiles = len(masks) - 1
    s = pl.ds(group * 8, 8)
    lane = lax.broadcasted_iota(jnp.int32, (8, LANES), 1)
    here = [src[row, t, s, :] for t in range(tiles + 1)]
    if ring is None:
        low, high = here[tiles], here[tiles]
    else:
        low, high = ring[0][row - 1, s, :], ring[1][row - 1, s, :]
    fwd = [pltpu.roll(h, NZ, 1) for h in here[:tiles] + [low]]
    bwd = [pltpu.roll(h, LANES - NZ, 1) for h in here[:tiles] + [high]]
    own = (fwd[tiles], bwd[tiles])
    if ring is not None:
        half = lane < LANES // 2
        own = (
            jnp.where(half, pltpu.roll(high, NZ, 1), fwd[tiles]),
            jnp.where(half, bwd[tiles], pltpu.roll(low, LANES - NZ, 1)),
        )
    one = [pltpu.roll(h, 1, 1) for h in here]
    neg = [pltpu.roll(h, LANES - 1, 1) for h in here]
    new = []
    for t in range(tiles if last else tiles + 1):
        before, after = (t - 1) % (tiles + 1), (t + 1) % (tiles + 1)
        mine = own if t == tiles else (fwd[t], bwd[t])
        beside = (src[row - 1, t, s, :] + src[row + 1, t, s, :]) + (
            jnp.where(lane < NZ, fwd[before], mine[0]) + jnp.where(lane >= LANES - NZ, bwd[after], mine[1])
        )
        starts = (t * LANES) % NZ == 0
        stops = ((t + 1) * LANES) % NZ == 0
        below = one[t] if starts else jnp.where(lane < 1, one[before], one[t])
        above = neg[t] if stops else jnp.where(lane >= LANES - 1, neg[after], neg[t])
        beside = beside + (masks[t][0] * below + masks[t][1] * above)
        new.append(coef[t][1] * here[t] + coef[t][0] * beside)
    return new


def step_kernel(batch, e0_in, hxa, hxb, hya, hyb, ub, s_gram, x3b, out, e0, e1, e2, low, high, acc_u, acc_x):
    cols = ub.shape[0]
    tiles = e0.shape[1] - 1
    odd_x = lax.rem(lax.axis_index("gx"), 2) == 1
    odd_y = lax.rem(lax.axis_index("gy"), 2) == 1
    lane = lax.broadcasted_iota(jnp.int32, (ROWS, LANES), 1)
    e0[0, tiles] = jnp.zeros((ROWS, LANES), F32)
    e0[cols + 2 * STEPS - 1, tiles] = jnp.zeros((ROWS, LANES), F32)

    def place_x(up, down):
        e0[0:STEPS, 0:tiles] = up[...]
        e0[cols + STEPS :, 0:tiles] = down[...]

    def place_y(lo, hi):
        for r in range(cols + 4):
            lo_row, hi_row = lo[r], hi[r]
            low[r] = lo_row
            high[r] = hi_row
            e0[r + 1, tiles] = jnp.where(lane < LANES // 2, hi_row, lo_row)

    pl.when(odd_x)(lambda: place_x(hxa, hxb))
    pl.when(jnp.logical_not(odd_x))(lambda: place_x(hxb, hxa))
    pl.when(odd_y)(lambda: place_y(hya, hyb))
    pl.when(jnp.logical_not(odd_y))(lambda: place_y(hyb, hya))
    masks = z_masks(tiles)

    @pl.loop(1, cols + 5)
    def _(row):
        coef = row_coef(e0, row, batch, tiles + 1)
        for group in range(4):
            for t, v in enumerate(step_row(e0, coef, row, group, masks, (low, high), False)):
                e1[row, t, pl.ds(group * 8, 8), :] = v

    @pl.loop(2, cols + 4)
    def _(row):
        coef = row_coef(e0, row, batch, tiles + 1)
        for group in range(4):
            for t, v in enumerate(step_row(e1, coef, row, group, masks, None, False)):
                e2[row, t, pl.ds(group * 8, 8), :] = v

    acc_u[...] = jnp.zeros_like(acc_u)
    acc_x[...] = jnp.zeros_like(acc_x)

    @pl.loop(0, cols)
    def _(i):
        coef = row_coef(e0, i + STEPS, batch, tiles)
        for pair in range(2):
            parts = [step_row(e2, coef, i + STEPS, 2 * pair + k, masks, None, True) for k in range(2)]
            for t in range(tiles):
                h, l = split(jnp.concatenate([parts[0][t], parts[1][t]], 0))
                x3b[i, pl.ds(pair * 16, 16), t * LANES : (t + 1) * LANES] = h
                x3b[i, pl.ds(ROWS + pair * 16, 16), t * LANES : (t + 1) * LANES] = l
        both = x3b[i]
        acc_u[...] += dot_t(ub[i], both)
        acc_x[...] += dot_t(both, both)

    count = ub.shape[1] // 2
    u = acc_u[0:count, :] + acc_u[count:, :]
    x = acc_x[0:ROWS, :] + acc_x[ROWS:, :]
    out[...] = jnp.zeros_like(out)
    out[:, 0:ROWS] = u[:, 0:ROWS] + u[:, ROWS:]
    out[0:ROWS, ROWS : 2 * ROWS] = x[:, 0:ROWS] + x[:, ROWS:]
    out[:, 2 * ROWS :] = s_gram[...]


def last_kernel(batch, cells, total, sigma, x3b, ub, basis, core, buf, sem):
    cols = x3b.shape[0]
    count = ub.shape[1] // 2
    inverse = 1.0 / cells
    col = lax.broadcasted_iota(jnp.int32, (count, ROWS), 1)
    c = jnp.where(col < batch, total[:, 0:ROWS], 0.0)
    rows = lax.broadcasted_iota(jnp.int32, (ROWS, ROWS), 0)
    lanes = lax.broadcasted_iota(jnp.int32, (ROWS, ROWS), 1)
    g = total[0:ROWS, ROWS : 2 * ROWS]
    s = total[:, 2 * ROWS :]
    first = c * inverse
    both = first + (c - small_dot(s, first)) * inverse
    rest = small_dot(s, both) - c
    gram = g - small_dot(c, both, ((0,), (0,))) + small_dot(both, rest, ((0,), (0,)))
    gram = jnp.where((rows < batch) & (lanes < batch), gram * inverse, jnp.where(rows == lanes, 1.0, 0.0))
    m = jnp.concatenate([gram, jnp.where(rows == lanes, 1.0, 0.0)], 1)
    wide = lax.broadcasted_iota(jnp.int32, (ROWS, 2 * ROWS), 0)
    scale = jnp.ones((ROWS, 1), F32)
    for j in range(batch):
        pivot = m[j : j + 1, :]
        d = pivot[:, j : j + 1]
        scale = jnp.where(wide[:, 0:1] == j, d, scale)
        factor = jnp.where(wide > j, m[:, j : j + 1] / d, 0.0)
        m = m - factor * pivot
    m = m * lax.rsqrt(scale)
    upper = jnp.where(rows <= lanes, m[:, 0:ROWS], 0.0)
    linv = m[:, ROWS:]
    wu = -small_dot(linv, both, ((1,), (1,)))
    core[...] = jnp.zeros_like(core)
    er = lax.broadcasted_iota(jnp.int32, (count, count), 0)
    ec = lax.broadcasted_iota(jnp.int32, (count, count), 1)
    core[0:count, 0:count] = jnp.where(er == ec, sigma[...], 0.0)
    core[0:count, count:] = both[:, 0:batch]
    core[count:, count:] = upper[0:batch, 0:batch]
    xh, xl = split(linv)
    uh, ul = split(wu)
    wx = jnp.concatenate([jnp.concatenate([xh, xh], 1), jnp.concatenate([xl, xl], 1)], 0)
    wm = jnp.concatenate([jnp.concatenate([uh, uh], 1), jnp.concatenate([ul, ul], 1)], 0)
    copies = []
    for i in range(cols):
        value = jnp.dot(wx, x3b[i], preferred_element_type=F32) + jnp.dot(wm, ub[i], preferred_element_type=F32)
        buf[i] = value[0:batch] + value[ROWS : ROWS + batch]
        copy = pltpu.make_async_copy(buf.at[i], basis.at[:, i, :], sem.at[i])
        copy.start()
        copies.append(copy)
    for copy in copies:
        copy.wait()


def in_hbm(value):
    return pltpu.with_memory_space_constraint(value, pltpu.HBM)


def swap(value, axis, offset):
    count = lax.axis_size(axis)
    pairs = [(i, i + 1) for i in range(offset, count - 1, 2)]
    return lax.ppermute(value, axis, pairs + [(j, i) for i, j in pairs])


def butterfly(value):
    for axis in ("gy", "gx"):
        count = lax.axis_size(axis)
        if count & (count - 1):
            value = lax.psum(value, axis)
            continue
        step = 1
        while step < count:
            value = value + lax.ppermute(value, axis, [(i, i ^ step) for i in range(count)])
            step *= 2
    return value


def body(snapshots, modes, mobility, phase, contact, sigma):
    batch, cols, width = snapshots.shape
    count = modes.shape[0]
    tiles = width // LANES
    vmem = pl.BlockSpec(memory_space=pltpu.VMEM)
    hbm = pl.BlockSpec(memory_space=pltpu.HBM)
    shape = jax.ShapeDtypeStruct
    params = pltpu.CompilerParams(vmem_limit_bytes=40 << 20)
    coef, zsa, zsb, sxa, sxb, sya, syb = pl.pallas_call(
        edge_kernel,
        out_shape=(shape((2, cols, width), F32),)
        + (shape((2, 2, ROWS, LANES), F32),) * 2
        + (shape((STEPS, tiles, ROWS, LANES), F32),) * 2
        + (shape((cols, ROWS, LANES), F32),) * 2,
        in_specs=[hbm] * 4,
        out_specs=(vmem,) * 7,
        scratch_shapes=[
            pltpu.VMEM((2 * STEPS, batch, width), F32),
            pltpu.VMEM((cols - 2 * STEPS, 2, batch, LANES), F32),
            pltpu.VMEM((cols, width), F32),
            pltpu.VMEM((cols, width), jnp.int32),
            pltpu.VMEM((cols, width), jnp.int32),
            pltpu.VMEM((2 * STEPS, tiles, ROWS, LANES), F32),
            pltpu.VMEM((2, cols, ROWS, LANES), F32),
            pltpu.SemaphoreType.DMA((2 * cols - 2 * STEPS,)),
            pltpu.SemaphoreType.DMA((3,)),
        ],
        compiler_params=params,
        name="edge",
    )(*(in_hbm(v) for v in (snapshots, mobility, phase, contact)))
    odd_x = lax.axis_index("gx") % 2 == 1
    odd_y = lax.axis_index("gy") % 2 == 1
    zra = swap(zsa, "gx", 0)
    zrb = swap(zsb, "gx", 1)
    hxa = swap(sxa, "gx", 0)
    hxb = swap(sxb, "gx", 1)
    up = jnp.where(odd_x, zra, zrb)
    down = jnp.where(odd_x, zrb, zra)

    def with_corners(own, low):
        return jnp.concatenate(
            [jnp.where(low, up[:, 0], up[:, 1]), own, jnp.where(low, down[:, 0], down[:, 1])], 0
        )

    hya = swap(with_corners(sya, odd_y), "gy", 0)
    hyb = swap(with_corners(syb, jnp.logical_not(odd_y)), "gy", 1)
    ext = (cols + 2 * STEPS, tiles + 1, ROWS, LANES)
    ub, s_gram, e0 = pl.pallas_call(
        modes_kernel,
        out_shape=(shape((cols, 2 * count, width), BF16), shape((count, count), F32), shape(ext, F32)),
        in_specs=[hbm, hbm, vmem],
        out_specs=(vmem,) * 3,
        scratch_shapes=[
            pltpu.VMEM((cols, count, width), F32),
            pltpu.VMEM((cols, batch, width), F32),
            pltpu.VMEM((2 * count, 2 * count), F32),
            pltpu.SemaphoreType.DMA((2 * cols,)),
        ],
        compiler_params=params,
        cost_estimate=pl.CostEstimate(flops=2 * cols * width * 4 * count * count, bytes_accessed=8 * cols * width * count, transcendentals=0),
        name="modes",
    )(in_hbm(modes), in_hbm(snapshots), coef)
    halo = pltpu.VMEM((cols + 4, ROWS, LANES), F32)
    x3b, part, _ = pl.pallas_call(
        lambda *refs: step_kernel(batch, *refs),
        out_shape=(shape((cols, 2 * ROWS, width), BF16), shape((count, LANES), F32), shape(ext, F32)),
        in_specs=[vmem] * 7,
        out_specs=(vmem,) * 3,
        scratch_shapes=[
            pltpu.VMEM(ext, F32),
            pltpu.VMEM(ext, F32),
            halo,
            halo,
            pltpu.VMEM((2 * count, 2 * ROWS), F32),
            pltpu.VMEM((2 * ROWS, 2 * ROWS), F32),
        ],
        input_output_aliases={0: 2},
        compiler_params=params,
        name="steps",
    )(e0, hxa, hxb, hya, hyb, ub, s_gram)
    total = butterfly(part)
    cells = float(cols * width * lax.axis_size("gx") * lax.axis_size("gy"))
    basis, core = pl.pallas_call(
        lambda *refs: last_kernel(batch, cells, *refs),
        out_shape=(shape(snapshots.shape, F32), shape((count + batch, count + batch), F32)),
        in_specs=[vmem] * 4,
        out_specs=(hbm, vmem),
        scratch_shapes=[pltpu.VMEM((cols, batch, width), F32), pltpu.SemaphoreType.DMA((cols,))],
        compiler_params=params,
        name="last",
    )(total, sigma.reshape(1, count), x3b, ub)
    return (basis, core)


def solution(mesh):
    return jax.shard_map(
        body,
        mesh=mesh,
        in_specs=(
            P(None, "gx", "gy"),
            P(None, "gx", "gy"),
            P("gx", "gy"),
            P("gx", "gy"),
            P("gx", "gy"),
            P(),
        ),
        out_specs=(P(None, "gx", "gy"), P()),
        check_vma=False,
    )
```

```python
import jax
import jax.numpy as jnp
from jax import lax
from jax.experimental import pallas as pl
from jax.experimental.pallas import tpu as pltpu
from jax.sharding import PartitionSpec as P

NZ = 24
STEPS = 3
LANES = 128
ROWS = 32
UNROLL = 2
HIGH = lax.Precision.HIGHEST
F32 = jnp.float32
BF16 = jnp.bfloat16


def split(value):
    high = value.astype(BF16)
    return high, (value - high.astype(F32)).astype(BF16)


def dot_t(a, b):
    return lax.dot_general(a, b, (((1,), (1,)), ((), ())), preferred_element_type=F32)


def small_dot(a, b, dims=((1,), (0,))):
    return lax.dot_general(a, b, (dims, ((), ())), precision=HIGH, preferred_element_type=F32)


def fill_rows(dst, index, fields, rate, keep):
    batch = fields.shape[0]
    dst[index + (pl.ds(0, batch),)] = fields
    dst[index + (pl.ds(batch, 1),)] = rate
    dst[index + (pl.ds(batch + 1, 1),)] = keep
    dst[index + (pl.ds(batch + 2, ROWS - batch - 2),)] = jnp.zeros((ROWS - batch - 2, LANES), F32)


def edge_kernel(snap, mob, pha, con, coef, sxa, sxb, sya, syb, bufx, bufy, vm, vp, vc, rows, cols_y, sem, sem_c):
    batch, cols, width = snap.shape
    tiles = width // LANES
    small = [
        pltpu.make_async_copy(ref, dst, sem_c.at[i])
        for i, (ref, dst) in enumerate(((mob, vm), (pha, vp), (con, vc)))
    ]
    outer = list(range(STEPS)) + list(range(cols - STEPS, cols))
    inner = list(range(STEPS, cols - STEPS))
    copies = [pltpu.make_async_copy(snap.at[:, i, :], bufx.at[k], sem.at[k]) for k, i in enumerate(outer)]
    for k, i in enumerate(inner):
        for side, start in enumerate((0, width - LANES)):
            n = len(outer) + 2 * k + side
            copies.append(
                pltpu.make_async_copy(snap.at[:, i, pl.ds(start, LANES)], bufy.at[k, side], sem.at[n])
            )
    for copy in small + copies:
        copy.start()
    for copy in small:
        copy.wait()
    rate = vm[...] * jnp.where(vp[...] == 1, 1.0, 0.5).astype(F32)
    lane = lax.broadcasted_iota(jnp.int32, (cols, width), 1) % NZ
    ends = jnp.where(lane == 0, 1.0, 0.0) + jnp.where(lane == NZ - 1, 1.0, 0.0)
    keep = 1.0 - 0.25 * vc[...].astype(F32) - rate * (6.0 - ends)
    coef[0] = rate
    coef[1] = keep
    for k, i in enumerate(outer):
        copies[k].wait()
        for t in range(tiles):
            span = slice(t * LANES, (t + 1) * LANES)
            fill_rows(rows, (k, t), bufx[k, :, span], rate[i : i + 1, span], keep[i : i + 1, span])
        for side, t in enumerate((0, tiles - 1)):
            cols_y[side, i] = rows[k, t]
    for k, i in enumerate(inner):
        for side, t in enumerate((0, tiles - 1)):
            copies[len(outer) + 2 * k + side].wait()
            span = slice(t * LANES, (t + 1) * LANES)
            fill_rows(cols_y, (side, i), bufy[k, side], rate[i : i + 1, span], keep[i : i + 1, span])
    odd_x = lax.rem(lax.axis_index("gx"), 2)
    odd_y = lax.rem(lax.axis_index("gy"), 2)
    sxa[...] = rows[pl.ds((1 - odd_x) * STEPS, STEPS)]
    sxb[...] = rows[pl.ds(odd_x * STEPS, STEPS)]
    sya[...] = cols_y[1 - odd_y]
    syb[...] = cols_y[odd_y]


def modes_kernel(modes, snap, coef, ub, gram, e0, buf, bufx, sem):
    count, cols, width = modes.shape
    batch = snap.shape[0]
    copies = [pltpu.make_async_copy(snap.at[:, i, :], bufx.at[i], sem.at[i]) for i in range(cols)]
    copies += [pltpu.make_async_copy(modes.at[:, i, :], buf.at[i], sem.at[cols + i]) for i in range(cols)]
    for copy in copies:
        copy.start()
    for i in range(cols):
        copies[i].wait()
        for t in range(width // LANES):
            span = slice(t * LANES, (t + 1) * LANES)
            fill_rows(e0, (i + STEPS, t), bufx[i, :, span], coef[0, i : i + 1, span], coef[1, i : i + 1, span])
    for i in range(cols):
        copies[cols + i].wait()
        high, low = split(buf[i])
        ub[i, 0:count, :] = high
        ub[i, count : 2 * count, :] = low
    acc = None
    for i in range(cols):
        part = dot_t(ub[i], ub[i, 0:count, :])
        acc = part if acc is None else acc + part
    cross = acc[count : 2 * count]
    gram[...] = acc[0:count] + (cross + cross.T)


def z_masks(tiles):
    lane = lax.broadcasted_iota(jnp.int32, (8, LANES), 1)
    found = []
    for t in range(tiles + 1):
        z = (lane + t * LANES) % NZ if t < tiles else jnp.where(lane < LANES // 2, lane % NZ, (lane + 16) % NZ)
        found.append((jnp.where(z == 0, 0.0, 1.0), jnp.where(z == NZ - 1, 0.0, 1.0)))
    return found


def row_coef(base, row, batch, tiles):
    return [
        [jnp.broadcast_to(base[row, t, pl.ds(batch + k, 1), :], (8, LANES)) for k in range(2)] for t in range(tiles)
    ]


def step_row(src, coef, row, group, masks, ring, last):
    tiles = len(masks) - 1
    s = pl.ds(group * 8, 8)
    lane = lax.broadcasted_iota(jnp.int32, (8, LANES), 1)
    here = [src[row, t, s, :] for t in range(tiles + 1)]
    if ring is None:
        low, high = here[tiles], here[tiles]
    else:
        low, high = ring[0][row - 1, s, :], ring[1][row - 1, s, :]
    fwd = [pltpu.roll(h, NZ, 1) for h in here[:tiles] + [low]]
    bwd = [pltpu.roll(h, LANES - NZ, 1) for h in here[:tiles] + [high]]
    own = (fwd[tiles], bwd[tiles])
    if ring is not None:
        half = lane < LANES // 2
        own = (
            jnp.where(half, pltpu.roll(high, NZ, 1), fwd[tiles]),
            jnp.where(half, bwd[tiles], pltpu.roll(low, LANES - NZ, 1)),
        )
    one = [pltpu.roll(h, 1, 1) for h in here]
    neg = [pltpu.roll(h, LANES - 1, 1) for h in here]
    new = []
    for t in range(tiles if last else tiles + 1):
        before, after = (t - 1) % (tiles + 1), (t + 1) % (tiles + 1)
        mine = own if t == tiles else (fwd[t], bwd[t])
        beside = (src[row - 1, t, s, :] + src[row + 1, t, s, :]) + (
            jnp.where(lane < NZ, fwd[before], mine[0]) + jnp.where(lane >= LANES - NZ, bwd[after], mine[1])
        )
        starts = (t * LANES) % NZ == 0
        stops = ((t + 1) * LANES) % NZ == 0
        below = one[t] if starts else jnp.where(lane < 1, one[before], one[t])
        above = neg[t] if stops else jnp.where(lane >= LANES - 1, neg[after], neg[t])
        beside = beside + (masks[t][0] * below + masks[t][1] * above)
        new.append(coef[t][1] * here[t] + coef[t][0] * beside)
    return new


def step_kernel(batch, e0_in, hxa, hxb, hya, hyb, ca, cb, ub, s_gram, x3b, out, e0, e1, e2, low, high):
    cols = ub.shape[0]
    tiles = e0.shape[1] - 1
    count = ub.shape[1] // 2
    odd_x = lax.rem(lax.axis_index("gx"), 2) == 1
    odd_y = lax.rem(lax.axis_index("gy"), 2) == 1
    lane = lax.broadcasted_iota(jnp.int32, (ROWS, LANES), 1)
    e0[0, tiles] = jnp.zeros((ROWS, LANES), F32)
    e0[cols + 2 * STEPS - 1, tiles] = jnp.zeros((ROWS, LANES), F32)

    def place_x(up, down):
        e0[0:STEPS, 0:tiles] = up[...]
        e0[cols + STEPS :, 0:tiles] = down[...]

    def place_y(lo, hi, lo_ends, hi_ends):
        for r in range(cols + 4):
            k = r - 2
            inside = 0 <= k < cols
            end = r if k < 0 else r - cols
            lo_row = lo[k] if inside else lo_ends[end]
            hi_row = hi[k] if inside else hi_ends[end]
            low[r] = lo_row
            high[r] = hi_row
            e0[r + 1, tiles] = jnp.where(lane < LANES // 2, hi_row, lo_row)

    pl.when(odd_x)(lambda: place_x(hxa, hxb))
    pl.when(jnp.logical_not(odd_x))(lambda: place_x(hxb, hxa))
    pl.when(odd_y)(lambda: place_y(hya, hyb, ca, cb))
    pl.when(jnp.logical_not(odd_y))(lambda: place_y(hyb, hya, cb, ca))
    masks = z_masks(tiles)

    def sweep(src, dst, start, stop, ring):
        @pl.loop(0, (stop - start) // UNROLL)
        def _(k):
            for j in range(UNROLL):
                row = start + k * UNROLL + j
                coef = row_coef(e0, row, batch, tiles + 1)
                for group in range(ROWS // 8):
                    for t, v in enumerate(step_row(src, coef, row, group, masks, ring, False)):
                        dst[row, t, pl.ds(group * 8, 8), :] = v

    sweep(e0, e1, 1, cols + 5, (low, high))
    sweep(e1, e2, 2, cols + 4, None)

    @pl.loop(0, cols // UNROLL)
    def _(k):
        for j in range(UNROLL):
            i = k * UNROLL + j
            coef = row_coef(e0, i + STEPS, batch, tiles)
            for pair in range(ROWS // 16):
                parts = [step_row(e2, coef, i + STEPS, 2 * pair + k, masks, None, True) for k in range(2)]
                for t in range(tiles):
                    h, l = split(jnp.concatenate([parts[0][t], parts[1][t]], 0))
                    x3b[i, pl.ds(pair * 16, 16), t * LANES : (t + 1) * LANES] = h
                    x3b[i, pl.ds(ROWS + pair * 16, 16), t * LANES : (t + 1) * LANES] = l

    acc_u = acc_x = None
    for i in range(cols):
        both = x3b[i]
        part_u, part_x = dot_t(ub[i], both), dot_t(both, both)
        acc_u = part_u if i == 0 else acc_u + part_u
        acc_x = part_x if i == 0 else acc_x + part_x
    u = acc_u[0:count, :] + acc_u[count:, :]
    x = acc_x[0:ROWS, :] + acc_x[ROWS:, :]
    out[...] = jnp.zeros_like(out)
    out[:, 0:ROWS] = u[:, 0:ROWS] + u[:, ROWS:]
    out[0:ROWS, ROWS : 2 * ROWS] = x[:, 0:ROWS] + x[:, ROWS:]
    out[:, 2 * ROWS :] = s_gram[...]


def last_kernel(batch, cells, total, sigma, x3b, ub, basis, core, buf, sem):
    cols = x3b.shape[0]
    count = ub.shape[1] // 2
    inverse = 1.0 / cells
    col = lax.broadcasted_iota(jnp.int32, (count, ROWS), 1)
    c = jnp.where(col < batch, total[:, 0:ROWS], 0.0)
    rows = lax.broadcasted_iota(jnp.int32, (ROWS, ROWS), 0)
    lanes = lax.broadcasted_iota(jnp.int32, (ROWS, ROWS), 1)
    g = total[0:ROWS, ROWS : 2 * ROWS]
    s = total[:, 2 * ROWS :]
    first = c * inverse
    both = first + (c - small_dot(s, first)) * inverse
    rest = small_dot(s, both) - c
    gram = g - small_dot(c, both, ((0,), (0,))) + small_dot(both, rest, ((0,), (0,)))
    gram = jnp.where((rows < batch) & (lanes < batch), gram * inverse, jnp.where(rows == lanes, 1.0, 0.0))
    m = jnp.concatenate([gram, jnp.where(rows == lanes, 1.0, 0.0)], 1)
    wide = lax.broadcasted_iota(jnp.int32, (ROWS, 2 * ROWS), 0)
    scale = jnp.ones((ROWS, 1), F32)
    for j in range(batch):
        pivot = m[j : j + 1, :]
        d = pivot[:, j : j + 1]
        scale = jnp.where(wide[:, 0:1] == j, d, scale)
        factor = jnp.where(wide > j, m[:, j : j + 1] / d, 0.0)
        m = m - factor * pivot
    m = m * lax.rsqrt(scale)
    upper = jnp.where(rows <= lanes, m[:, 0:ROWS], 0.0)
    linv = m[:, ROWS:]
    wu = -small_dot(linv, both, ((1,), (1,)))
    core[...] = jnp.zeros_like(core)
    er = lax.broadcasted_iota(jnp.int32, (count, count), 0)
    ec = lax.broadcasted_iota(jnp.int32, (count, count), 1)
    core[0:count, 0:count] = jnp.where(er == ec, sigma[...], 0.0)
    core[0:count, count:] = both[:, 0:batch]
    core[count:, count:] = upper[0:batch, 0:batch]
    xh, xl = split(linv)
    uh, ul = split(wu)
    wx = jnp.concatenate([jnp.concatenate([xh, xh], 1), jnp.concatenate([xl, xl], 1)], 0)
    wm = jnp.concatenate([jnp.concatenate([uh, uh], 1), jnp.concatenate([ul, ul], 1)], 0)
    copies = []
    for i in range(cols):
        value = jnp.dot(wx, x3b[i], preferred_element_type=F32) + jnp.dot(wm, ub[i], preferred_element_type=F32)
        buf[i] = value[0:batch] + value[ROWS : ROWS + batch]
        copy = pltpu.make_async_copy(buf.at[i], basis.at[:, i, :], sem.at[i])
        copy.start()
        copies.append(copy)
    for copy in copies:
        copy.wait()


def in_hbm(value):
    return pltpu.with_memory_space_constraint(value, pltpu.HBM)


def swap(value, axis, offset):
    count = lax.axis_size(axis)
    pairs = [(i, i + 1) for i in range(offset, count - 1, 2)]
    return lax.ppermute(value, axis, pairs + [(j, i) for i, j in pairs])


def butterfly(value):
    for axis in ("gy", "gx"):
        count = lax.axis_size(axis)
        if count & (count - 1):
            value = lax.psum(value, axis)
            continue
        step = 1
        while step < count:
            value = value + lax.ppermute(value, axis, [(i, i ^ step) for i in range(count)])
            step *= 2
    return value


def body(snapshots, modes, mobility, phase, contact, sigma):
    batch, cols, width = snapshots.shape
    count = modes.shape[0]
    tiles = width // LANES
    vmem = pl.BlockSpec(memory_space=pltpu.VMEM)
    hbm = pl.BlockSpec(memory_space=pltpu.HBM)
    shape = jax.ShapeDtypeStruct
    params = pltpu.CompilerParams(vmem_limit_bytes=40 << 20)
    coef, sxa, sxb, sya, syb = pl.pallas_call(
        edge_kernel,
        out_shape=(shape((2, cols, width), F32),)
        + (shape((STEPS, tiles, ROWS, LANES), F32),) * 2
        + (shape((cols, ROWS, LANES), F32),) * 2,
        in_specs=[hbm] * 4,
        out_specs=(vmem,) * 5,
        scratch_shapes=[
            pltpu.VMEM((2 * STEPS, batch, width), F32),
            pltpu.VMEM((cols - 2 * STEPS, 2, batch, LANES), F32),
            pltpu.VMEM((cols, width), F32),
            pltpu.VMEM((cols, width), jnp.int32),
            pltpu.VMEM((cols, width), jnp.int32),
            pltpu.VMEM((2 * STEPS, tiles, ROWS, LANES), F32),
            pltpu.VMEM((2, cols, ROWS, LANES), F32),
            pltpu.SemaphoreType.DMA((2 * cols - 2 * STEPS,)),
            pltpu.SemaphoreType.DMA((3,)),
        ],
        compiler_params=params,
        name="edge",
    )(*(in_hbm(v) for v in (snapshots, mobility, phase, contact)))
    odd_x = lax.axis_index("gx") % 2 == 1
    odd_y = lax.axis_index("gy") % 2 == 1
    hxa = swap(sxa, "gx", 0)
    hxb = swap(sxb, "gx", 1)
    hya = swap(sya, "gy", 0)
    hyb = swap(syb, "gy", 1)
    ext = (cols + 2 * STEPS, tiles + 1, ROWS, LANES)
    ub, s_gram, e0 = pl.pallas_call(
        modes_kernel,
        out_shape=(shape((cols, 2 * count, width), BF16), shape((count, count), F32), shape(ext, F32)),
        in_specs=[hbm, hbm, vmem],
        out_specs=(vmem,) * 3,
        scratch_shapes=[
            pltpu.VMEM((cols, count, width), F32),
            pltpu.VMEM((cols, batch, width), F32),
            pltpu.SemaphoreType.DMA((2 * cols,)),
        ],
        compiler_params=params,
        cost_estimate=pl.CostEstimate(flops=2 * cols * width * 4 * count * count, bytes_accessed=8 * cols * width * count, transcendentals=0),
        name="modes",
    )(in_hbm(modes), in_hbm(snapshots), coef)
    hxa, hxb, s_gram = lax.optimization_barrier((hxa, hxb, s_gram))

    def corners(low_side):
        side = [jnp.where(low_side, h[:, 0], h[:, tiles - 1]) for h in (hxa, hxb)]
        up = jnp.where(odd_x, side[0][1:], side[1][1:])
        down = jnp.where(odd_x, side[1][:2], side[0][:2])
        return jnp.concatenate([up, down], 0)

    ca = swap(corners(odd_y), "gy", 0)
    cb = swap(corners(jnp.logical_not(odd_y)), "gy", 1)
    halo = pltpu.VMEM((cols + 4, ROWS, LANES), F32)
    x3b, part, _ = pl.pallas_call(
        lambda *refs: step_kernel(batch, *refs),
        out_shape=(shape((cols, 2 * ROWS, width), BF16), shape((count, LANES), F32), shape(ext, F32)),
        in_specs=[vmem] * 9,
        out_specs=(vmem,) * 3,
        scratch_shapes=[
            pltpu.VMEM(ext, F32),
            pltpu.VMEM(ext, F32),
            halo,
            halo,
        ],
        input_output_aliases={0: 2},
        compiler_params=params,
        name="steps",
    )(e0, hxa, hxb, hya, hyb, ca, cb, ub, s_gram)
    total = butterfly(part)
    cells = float(cols * width * lax.axis_size("gx") * lax.axis_size("gy"))
    basis, core = pl.pallas_call(
        lambda *refs: last_kernel(batch, cells, *refs),
        out_shape=(shape(snapshots.shape, F32), shape((count + batch, count + batch), F32)),
        in_specs=[vmem] * 4,
        out_specs=(hbm, vmem),
        scratch_shapes=[pltpu.VMEM((cols, batch, width), F32), pltpu.SemaphoreType.DMA((cols,))],
        compiler_params=params,
        name="last",
    )(total, sigma.reshape(1, count), x3b, ub)
    return (basis, core)


def solution(mesh):
    return jax.shard_map(
        body,
        mesh=mesh,
        in_specs=(
            P(None, "gx", "gy"),
            P(None, "gx", "gy"),
            P("gx", "gy"),
            P("gx", "gy"),
            P("gx", "gy"),
            P(),
        ),
        out_specs=(P(None, "gx", "gy"), P()),
        check_vma=False,
    )
```

```python
import jax
import jax.numpy as jnp
from jax import lax
from jax.experimental import pallas as pl
from jax.experimental.pallas import tpu as pltpu
from jax.sharding import PartitionSpec as P

NZ = 24
STEPS = 3
LANES = 128
ROWS = 32
UNROLL = 6
GROUP = 8
HIGH = lax.Precision.HIGHEST
F32 = jnp.float32
BF16 = jnp.bfloat16


def split(value):
    high = value.astype(BF16)
    return high, (value - high.astype(F32)).astype(BF16)


def dot_t(a, b):
    return lax.dot_general(a, b, (((1,), (1,)), ((), ())), preferred_element_type=F32)


def small_dot(a, b, dims=((1,), (0,))):
    return lax.dot_general(a, b, (dims, ((), ())), precision=HIGH, preferred_element_type=F32)


def fill_rows(dst, index, fields, rate, keep):
    batch = fields.shape[0]
    dst[index + (pl.ds(0, batch),)] = fields
    dst[index + (pl.ds(batch, 1),)] = rate
    dst[index + (pl.ds(batch + 1, 1),)] = keep
    dst[index + (pl.ds(batch + 2, ROWS - batch - 2),)] = jnp.zeros((ROWS - batch - 2, LANES), F32)


def edge_kernel(snap, mob, pha, con, coef, sxa, sxb, sya, syb, bufx, bufy, vm, vp, vc, rows, cols_y, sem, sem_c):
    batch, cols, width = snap.shape
    tiles = width // LANES
    small = [
        pltpu.make_async_copy(ref, dst, sem_c.at[i])
        for i, (ref, dst) in enumerate(((mob, vm), (pha, vp), (con, vc)))
    ]
    outer = list(range(STEPS)) + list(range(cols - STEPS, cols))
    inner = list(range(STEPS, cols - STEPS))
    copies = [pltpu.make_async_copy(snap.at[:, i, :], bufx.at[k], sem.at[k]) for k, i in enumerate(outer)]
    for k, i in enumerate(inner):
        for side, start in enumerate((0, width - LANES)):
            n = len(outer) + 2 * k + side
            copies.append(
                pltpu.make_async_copy(snap.at[:, i, pl.ds(start, LANES)], bufy.at[k, side], sem.at[n])
            )
    for copy in small + copies:
        copy.start()
    for copy in small:
        copy.wait()
    rate = vm[...] * jnp.where(vp[...] == 1, 1.0, 0.5).astype(F32)
    lane = lax.broadcasted_iota(jnp.int32, (cols, width), 1) % NZ
    ends = jnp.where(lane == 0, 1.0, 0.0) + jnp.where(lane == NZ - 1, 1.0, 0.0)
    keep = 1.0 - 0.25 * vc[...].astype(F32) - rate * (6.0 - ends)
    coef[0] = rate
    coef[1] = keep
    for k, i in enumerate(outer):
        copies[k].wait()
        for t in range(tiles):
            span = slice(t * LANES, (t + 1) * LANES)
            fill_rows(rows, (k, t), bufx[k, :, span], rate[i : i + 1, span], keep[i : i + 1, span])
        for side, t in enumerate((0, tiles - 1)):
            cols_y[side, i] = rows[k, t]
    for k, i in enumerate(inner):
        for side, t in enumerate((0, tiles - 1)):
            copies[len(outer) + 2 * k + side].wait()
            span = slice(t * LANES, (t + 1) * LANES)
            fill_rows(cols_y, (side, i), bufy[k, side], rate[i : i + 1, span], keep[i : i + 1, span])
    odd_x = lax.rem(lax.axis_index("gx"), 2)
    odd_y = lax.rem(lax.axis_index("gy"), 2)
    sxa[...] = rows[pl.ds((1 - odd_x) * STEPS, STEPS)]
    sxb[...] = rows[pl.ds(odd_x * STEPS, STEPS)]
    sya[...] = cols_y[1 - odd_y]
    syb[...] = cols_y[odd_y]


def modes_kernel(modes, snap, coef, xu, gram, e0, buf, bufx, sem):
    count, cols, width = modes.shape
    batch = snap.shape[0]
    copies = [pltpu.make_async_copy(snap.at[:, i, :], bufx.at[i], sem.at[i]) for i in range(cols)]
    copies += [pltpu.make_async_copy(modes.at[:, i, :], buf.at[i], sem.at[cols + i]) for i in range(cols)]
    for copy in copies:
        copy.start()
    for i in range(cols):
        copies[i].wait()
        for t in range(width // LANES):
            span = slice(t * LANES, (t + 1) * LANES)
            fill_rows(e0, (i + STEPS, t), bufx[i, :, span], coef[0, i : i + 1, span], coef[1, i : i + 1, span])
    for i in range(cols):
        copies[cols + i].wait()
        high, low = split(buf[i])
        xu[i, 0:count, :] = high
        xu[i, count : 2 * count, :] = low
    acc = None
    for i in range(cols):
        part = dot_t(xu[i, 0 : 2 * count, :], xu[i, 0:count, :])
        acc = part if acc is None else acc + part
    cross = acc[count : 2 * count]
    gram[...] = acc[0:count] + (cross + cross.T)


def z_masks(tiles):
    lane = lax.broadcasted_iota(jnp.int32, (8, LANES), 1)
    found = []
    for t in range(tiles + 1):
        z = (lane + t * LANES) % NZ if t < tiles else jnp.where(lane < LANES // 2, lane % NZ, (lane + 16) % NZ)
        found.append((jnp.where(z == 0, 0.0, 1.0), jnp.where(z == NZ - 1, 0.0, 1.0)))
    return found


def row_coef(base, row, batch, tiles):
    return [
        [jnp.broadcast_to(base[row, t, pl.ds(batch + k, 1), :], (8, LANES)) for k in range(2)] for t in range(tiles)
    ]


def step_row(src, coef, row, group, masks, ring, last):
    tiles = len(masks) - 1
    s = pl.ds(group * 8, 8)
    lane = lax.broadcasted_iota(jnp.int32, (8, LANES), 1)
    here = [src[row, t, s, :] for t in range(tiles + 1)]
    if ring is None:
        low, high = here[tiles], here[tiles]
    else:
        low, high = ring[0][row - 1, s, :], ring[1][row - 1, s, :]
    fwd = [pltpu.roll(h, NZ, 1) for h in here[:tiles] + [low]]
    bwd = [pltpu.roll(h, LANES - NZ, 1) for h in here[:tiles] + [high]]
    own = (fwd[tiles], bwd[tiles])
    if ring is not None:
        half = lane < LANES // 2
        own = (
            jnp.where(half, pltpu.roll(high, NZ, 1), fwd[tiles]),
            jnp.where(half, bwd[tiles], pltpu.roll(low, LANES - NZ, 1)),
        )
    one = [pltpu.roll(h, 1, 1) for h in here]
    neg = [pltpu.roll(h, LANES - 1, 1) for h in here]
    new = []
    for t in range(tiles if last else tiles + 1):
        before, after = (t - 1) % (tiles + 1), (t + 1) % (tiles + 1)
        mine = own if t == tiles else (fwd[t], bwd[t])
        beside = (src[row - 1, t, s, :] + src[row + 1, t, s, :]) + (
            jnp.where(lane < NZ, fwd[before], mine[0]) + jnp.where(lane >= LANES - NZ, bwd[after], mine[1])
        )
        starts = (t * LANES) % NZ == 0
        stops = ((t + 1) * LANES) % NZ == 0
        below = one[t] if starts else jnp.where(lane < 1, one[before], one[t])
        above = neg[t] if stops else jnp.where(lane >= LANES - 1, neg[after], neg[t])
        beside = beside + (masks[t][0] * below + masks[t][1] * above)
        new.append(coef[t][1] * here[t] + coef[t][0] * beside)
    return new


def step_kernel(batch, e0_in, xu_in, hxa, hxb, hya, hyb, ca, cb, s_gram, out, e0, xu, e1, e2, low, high):
    cols = xu.shape[0]
    tiles = e0.shape[1] - 1
    count = xu.shape[1] // 2 - ROWS
    base = 2 * count
    odd_x = lax.rem(lax.axis_index("gx"), 2) == 1
    odd_y = lax.rem(lax.axis_index("gy"), 2) == 1
    lane = lax.broadcasted_iota(jnp.int32, (ROWS, LANES), 1)
    e0[0, tiles] = jnp.zeros((ROWS, LANES), F32)
    e0[cols + 2 * STEPS - 1, tiles] = jnp.zeros((ROWS, LANES), F32)

    def place_x(up, down):
        e0[0:STEPS, 0:tiles] = up[...]
        e0[cols + STEPS :, 0:tiles] = down[...]

    def place_y(lo, hi, lo_ends, hi_ends):
        for r in range(cols + 4):
            k = r - 2
            inside = 0 <= k < cols
            end = r if k < 0 else r - cols
            lo_row = lo[k] if inside else lo_ends[end]
            hi_row = hi[k] if inside else hi_ends[end]
            low[r] = lo_row
            high[r] = hi_row
            e0[r + 1, tiles] = jnp.where(lane < LANES // 2, hi_row, lo_row)

    pl.when(odd_x)(lambda: place_x(hxa, hxb))
    pl.when(jnp.logical_not(odd_x))(lambda: place_x(hxb, hxa))
    pl.when(odd_y)(lambda: place_y(hya, hyb, ca, cb))
    pl.when(jnp.logical_not(odd_y))(lambda: place_y(hyb, hya, cb, ca))
    masks = z_masks(tiles)

    def sweep(src, dst, start, stop, ring):
        unroll = max(u for u in range(1, UNROLL + 1) if (stop - start) % u == 0)

        @pl.loop(0, (stop - start) // unroll)
        def _(k):
            for j in range(unroll):
                row = start + k * unroll + j
                coef = row_coef(e0, row, batch, tiles + 1)
                for group in range(ROWS // 8):
                    for t, v in enumerate(step_row(src, coef, row, group, masks, ring, False)):
                        dst[row, t, pl.ds(group * 8, 8), :] = v

    sweep(e0, e1, 1, cols + 5, (low, high))
    sweep(e1, e2, 2, cols + 4, None)

    @pl.loop(0, cols // 4)
    def _(k):
        for j in range(4):
            i = k * 4 + j
            coef = row_coef(e0, i + STEPS, batch, tiles)
            for pair in range(ROWS // 16):
                parts = [step_row(e2, coef, i + STEPS, 2 * pair + k, masks, None, True) for k in range(2)]
                for t in range(tiles):
                    h, l = split(jnp.concatenate([parts[0][t], parts[1][t]], 0))
                    xu[i, pl.ds(base + pair * 16, 16), t * LANES : (t + 1) * LANES] = h
                    xu[i, pl.ds(base + ROWS + pair * 16, 16), t * LANES : (t + 1) * LANES] = l

    acc = None
    for i in range(cols):
        part = dot_t(xu[i], xu[i, base:, :])
        acc = part if acc is None else acc + part
    u = acc[0:count, :] + acc[count:base, :]
    x = acc[base : base + ROWS, :] + acc[base + ROWS :, :]
    u = u[:, 0:ROWS] + u[:, ROWS:]
    s = s_gram[...]
    half = count // 2
    quarter = half // 2
    x = x[:, 0:ROWS] + x[:, ROWS:]
    out[0:half, :] = jnp.concatenate([u[0:half], u[half:], x, s[0:half, half:]], 1)
    corner = [s[k * half : (k + 1) * half, k * half : (k + 1) * half] for k in range(2)]
    out[half:, :] = jnp.concatenate([c[k * quarter : (k + 1) * quarter] for c in corner for k in range(2)], 1)


def last_kernel(batch, cells, total, sigma, xu, basis, core, buf, sem):
    cols = xu.shape[0]
    count = xu.shape[1] // 2 - ROWS
    half = count // 2
    inverse = 1.0 / cells
    blocks = [total[0:half, k * half : (k + 1) * half] for k in range(4)]
    pieces = [total[half:, k * half : (k + 1) * half] for k in range(4)]
    col = lax.broadcasted_iota(jnp.int32, (count, ROWS), 1)
    c = jnp.where(col < batch, jnp.concatenate(blocks[:2], 0), 0.0)
    rows = lax.broadcasted_iota(jnp.int32, (ROWS, ROWS), 0)
    lanes = lax.broadcasted_iota(jnp.int32, (ROWS, ROWS), 1)
    g = blocks[2]
    s = jnp.concatenate(
        [
            jnp.concatenate([jnp.concatenate(pieces[:2], 0), blocks[3]], 1),
            jnp.concatenate([blocks[3].T, jnp.concatenate(pieces[2:], 0)], 1),
        ],
        0,
    )
    first = c * inverse
    both = first + (c - small_dot(s, first)) * inverse
    rest = small_dot(s, both) - c
    gram = g - small_dot(c, both, ((0,), (0,))) + small_dot(both, rest, ((0,), (0,)))
    gram = jnp.where((rows < batch) & (lanes < batch), gram * inverse, jnp.where(rows == lanes, 1.0, 0.0))
    m = jnp.concatenate([gram, jnp.where(rows == lanes, 1.0, 0.0)], 1)
    index = lax.broadcasted_iota(jnp.int32, (ROWS, 1), 0)
    scale = jnp.ones((ROWS, 2 * ROWS), F32)
    for j in range(batch):
        pivot = m[j : j + 1, :]
        column = jnp.broadcast_to(m[:, j : j + 1], m.shape)
        d = column[j : j + 1, :]
        scale = jnp.where(index == j, d, scale)
        m = m - jnp.where(index > j, column, 0.0) * (pivot * (1.0 / d))
    m = m * lax.rsqrt(scale)
    upper = jnp.where(rows <= lanes, m[:, 0:ROWS], 0.0)
    linv = m[:, ROWS:]
    wu = -small_dot(linv, both, ((1,), (1,)))
    xh, xl = split(linv)
    uh, ul = split(wu)
    w = jnp.concatenate(
        [jnp.concatenate([uh, uh, xh, xh], 1), jnp.concatenate([ul, ul, xl, xl], 1)], 0
    )
    copies = [pltpu.make_async_copy(buf.at[i], basis.at[:, i, :], sem.at[i]) for i in range(cols)]
    for start in range(0, cols, GROUP):
        for i in range(start, start + GROUP):
            value = jnp.dot(w, xu[i], preferred_element_type=F32)
            buf[i] = value[0:batch] + value[ROWS : ROWS + batch]
        for i in range(start, start + GROUP):
            copies[i].start()
    core[...] = jnp.zeros_like(core)
    er = lax.broadcasted_iota(jnp.int32, (count, count), 0)
    ec = lax.broadcasted_iota(jnp.int32, (count, count), 1)
    core[0:count, 0:count] = jnp.where(er == ec, sigma[...], 0.0)
    core[0:count, count:] = both[:, 0:batch]
    core[count:, count:] = upper[0:batch, 0:batch]
    for copy in copies:
        copy.wait()


def in_hbm(value):
    return pltpu.with_memory_space_constraint(value, pltpu.HBM)


def swap(value, axis, offset):
    count = lax.axis_size(axis)
    pairs = [(i, i + 1) for i in range(offset, count - 1, 2)]
    return lax.ppermute(value, axis, pairs + [(j, i) for i, j in pairs])


def butterfly(value):
    for axis in ("gy", "gx"):
        count = lax.axis_size(axis)
        if count & (count - 1):
            value = lax.psum(value, axis)
            continue
        step = 1
        while step < count:
            value = value + lax.ppermute(value, axis, [(i, i ^ step) for i in range(count)])
            step *= 2
    return value


def body(snapshots, modes, mobility, phase, contact, sigma):
    batch, cols, width = snapshots.shape
    count = modes.shape[0]
    tiles = width // LANES
    vmem = pl.BlockSpec(memory_space=pltpu.VMEM)
    hbm = pl.BlockSpec(memory_space=pltpu.HBM)
    shape = jax.ShapeDtypeStruct
    params = pltpu.CompilerParams(vmem_limit_bytes=40 << 20)
    coef, sxa, sxb, sya, syb = pl.pallas_call(
        edge_kernel,
        out_shape=(shape((2, cols, width), F32),)
        + (shape((STEPS, tiles, ROWS, LANES), F32),) * 2
        + (shape((cols, ROWS, LANES), F32),) * 2,
        in_specs=[hbm] * 4,
        out_specs=(vmem,) * 5,
        scratch_shapes=[
            pltpu.VMEM((2 * STEPS, batch, width), F32),
            pltpu.VMEM((cols - 2 * STEPS, 2, batch, LANES), F32),
            pltpu.VMEM((cols, width), F32),
            pltpu.VMEM((cols, width), jnp.int32),
            pltpu.VMEM((cols, width), jnp.int32),
            pltpu.VMEM((2 * STEPS, tiles, ROWS, LANES), F32),
            pltpu.VMEM((2, cols, ROWS, LANES), F32),
            pltpu.SemaphoreType.DMA((2 * cols - 2 * STEPS,)),
            pltpu.SemaphoreType.DMA((3,)),
        ],
        compiler_params=params,
        name="edge",
    )(*(in_hbm(v) for v in (snapshots, mobility, phase, contact)))
    odd_x = lax.axis_index("gx") % 2 == 1
    odd_y = lax.axis_index("gy") % 2 == 1
    hxa = swap(sxa, "gx", 0)
    hxb = swap(sxb, "gx", 1)
    hya = swap(sya, "gy", 0)
    hyb = swap(syb, "gy", 1)
    ext = (cols + 2 * STEPS, tiles + 1, ROWS, LANES)
    xu, s_gram, e0 = pl.pallas_call(
        modes_kernel,
        out_shape=(shape((cols, 2 * (count + ROWS), width), BF16), shape((count, count), F32), shape(ext, F32)),
        in_specs=[hbm, hbm, vmem],
        out_specs=(vmem,) * 3,
        scratch_shapes=[
            pltpu.VMEM((cols, count, width), F32),
            pltpu.VMEM((cols, batch, width), F32),
            pltpu.SemaphoreType.DMA((2 * cols,)),
        ],
        compiler_params=params,
        cost_estimate=pl.CostEstimate(flops=2 * cols * width * 4 * count * count, bytes_accessed=8 * cols * width * count, transcendentals=0),
        name="modes",
    )(in_hbm(modes), in_hbm(snapshots), coef)
    hxa, hxb, s_gram = lax.optimization_barrier((hxa, hxb, s_gram))

    def corners(low_side):
        side = [jnp.where(low_side, h[:, 0], h[:, tiles - 1]) for h in (hxa, hxb)]
        up = jnp.where(odd_x, side[0][1:], side[1][1:])
        down = jnp.where(odd_x, side[1][:2], side[0][:2])
        return jnp.concatenate([up, down], 0)

    ca = swap(corners(odd_y), "gy", 0)
    cb = swap(corners(jnp.logical_not(odd_y)), "gy", 1)
    halo = pltpu.VMEM((cols + 4, ROWS, LANES), F32)
    part, _, xu = pl.pallas_call(
        lambda *refs: step_kernel(batch, *refs),
        out_shape=(
            shape((3 * count // 4, 2 * count), F32),
            shape(ext, F32),
            shape((cols, 2 * (count + ROWS), width), BF16),
        ),
        in_specs=[vmem] * 9,
        out_specs=(vmem,) * 3,
        scratch_shapes=[
            pltpu.VMEM(ext, F32),
            pltpu.VMEM(ext, F32),
            halo,
            halo,
        ],
        input_output_aliases={0: 1, 1: 2},
        compiler_params=params,
        name="steps",
    )(e0, xu, hxa, hxb, hya, hyb, ca, cb, s_gram)
    total = butterfly(part)
    cells = float(cols * width * lax.axis_size("gx") * lax.axis_size("gy"))
    basis, core = pl.pallas_call(
        lambda *refs: last_kernel(batch, cells, *refs),
        out_shape=(shape(snapshots.shape, F32), shape((count + batch, count + batch), F32)),
        in_specs=[vmem] * 3,
        out_specs=(hbm, vmem),
        scratch_shapes=[pltpu.VMEM((cols, batch, width), F32), pltpu.SemaphoreType.DMA((cols,))],
        compiler_params=params,
        name="last",
    )(total, sigma.reshape(1, count), xu)
    return (basis, core)


def solution(mesh):
    return jax.shard_map(
        body,
        mesh=mesh,
        in_specs=(
            P(None, "gx", "gy"),
            P(None, "gx", "gy"),
            P("gx", "gy"),
            P("gx", "gy"),
            P("gx", "gy"),
            P(),
        ),
        out_specs=(P(None, "gx", "gy"), P()),
        check_vma=False,
    )
```

```python
import jax
import jax.numpy as jnp
from jax import lax
from jax.experimental import pallas as pl
from jax.experimental.pallas import tpu as pltpu
from jax.sharding import PartitionSpec as P

NZ = 24
STEPS = 3
LANES = 128
ROWS = 32
UNROLL = 6
GROUP = 8
HIGH = lax.Precision.HIGHEST
F32 = jnp.float32
BF16 = jnp.bfloat16


def split(value):
    high = value.astype(BF16)
    return high, (value - high.astype(F32)).astype(BF16)


def dot_t(a, b):
    return lax.dot_general(a, b, (((1,), (1,)), ((), ())), preferred_element_type=F32)


def small_dot(a, b, dims=((1,), (0,))):
    return lax.dot_general(a, b, (dims, ((), ())), precision=HIGH, preferred_element_type=F32)


def fill_rows(dst, index, fields, rate, keep):
    batch = fields.shape[0]
    dst[index + (pl.ds(0, batch),)] = fields
    dst[index + (pl.ds(batch, 1),)] = rate
    dst[index + (pl.ds(batch + 1, 1),)] = keep
    dst[index + (pl.ds(batch + 2, ROWS - batch - 2),)] = jnp.zeros((ROWS - batch - 2, LANES), F32)


def edge_kernel(snap, mob, pha, con, coef, sxa, sxb, sya, syb, bufx, bufy, vm, vp, vc, rows, cols_y, sem, sem_c):
    batch, cols, width = snap.shape
    tiles = width // LANES
    small = [
        pltpu.make_async_copy(ref, dst, sem_c.at[i])
        for i, (ref, dst) in enumerate(((mob, vm), (pha, vp), (con, vc)))
    ]
    outer = list(range(STEPS)) + list(range(cols - STEPS, cols))
    inner = list(range(STEPS, cols - STEPS))
    copies = [pltpu.make_async_copy(snap.at[:, i, :], bufx.at[k], sem.at[k]) for k, i in enumerate(outer)]
    for k, i in enumerate(inner):
        for side, start in enumerate((0, width - LANES)):
            n = len(outer) + 2 * k + side
            copies.append(
                pltpu.make_async_copy(snap.at[:, i, pl.ds(start, LANES)], bufy.at[k, side], sem.at[n])
            )
    for copy in small + copies:
        copy.start()
    for copy in small:
        copy.wait()
    rate = vm[...] * jnp.where(vp[...] == 1, 1.0, 0.5).astype(F32)
    lane = lax.broadcasted_iota(jnp.int32, (cols, width), 1) % NZ
    ends = jnp.where(lane == 0, 1.0, 0.0) + jnp.where(lane == NZ - 1, 1.0, 0.0)
    keep = 1.0 - 0.25 * vc[...].astype(F32) - rate * (6.0 - ends)
    coef[0] = rate
    coef[1] = keep
    for k, i in enumerate(outer):
        copies[k].wait()
        for t in range(tiles):
            span = slice(t * LANES, (t + 1) * LANES)
            fill_rows(rows, (k, t), bufx[k, :, span], rate[i : i + 1, span], keep[i : i + 1, span])
        for side, t in enumerate((0, tiles - 1)):
            cols_y[side, i] = rows[k, t]
    for k, i in enumerate(inner):
        for side, t in enumerate((0, tiles - 1)):
            copies[len(outer) + 2 * k + side].wait()
            span = slice(t * LANES, (t + 1) * LANES)
            fill_rows(cols_y, (side, i), bufy[k, side], rate[i : i + 1, span], keep[i : i + 1, span])
    odd_x = lax.rem(lax.axis_index("gx"), 2)
    odd_y = lax.rem(lax.axis_index("gy"), 2)
    sxa[...] = rows[pl.ds((1 - odd_x) * STEPS, STEPS)]
    sxb[...] = rows[pl.ds(odd_x * STEPS, STEPS)]
    sya[...] = cols_y[1 - odd_y]
    syb[...] = cols_y[odd_y]


def modes_kernel(modes, snap, coef, xu, gram, e0, buf, bufx, sem):
    count, cols, width = modes.shape
    batch = snap.shape[0]
    copies = [pltpu.make_async_copy(snap.at[:, i, :], bufx.at[i], sem.at[i]) for i in range(cols)]
    copies += [pltpu.make_async_copy(modes.at[:, i, :], buf.at[i], sem.at[cols + i]) for i in range(cols)]
    for copy in copies:
        copy.start()
    for i in range(cols):
        copies[i].wait()
        for t in range(width // LANES):
            span = slice(t * LANES, (t + 1) * LANES)
            fill_rows(e0, (i + STEPS, t), bufx[i, :, span], coef[0, i : i + 1, span], coef[1, i : i + 1, span])
    for i in range(cols):
        copies[cols + i].wait()
        high, low = split(buf[i])
        xu[i, 0:count, :] = high
        xu[i, count : 2 * count, :] = low
    acc = None
    for i in range(cols):
        part = dot_t(xu[i, 0 : 2 * count, :], xu[i, 0:count, :])
        acc = part if acc is None else acc + part
    cross = acc[count : 2 * count]
    gram[...] = acc[0:count] + (cross + cross.T)


def z_masks(tiles):
    lane = lax.broadcasted_iota(jnp.int32, (8, LANES), 1)
    found = []
    for t in range(tiles + 1):
        z = (lane + t * LANES) % NZ if t < tiles else jnp.where(lane < LANES // 2, lane % NZ, (lane + 16) % NZ)
        found.append((jnp.where(z == 0, 0.0, 1.0), jnp.where(z == NZ - 1, 0.0, 1.0)))
    return found


def row_coef(base, row, batch, tiles):
    return [
        [jnp.broadcast_to(base[row, t, pl.ds(batch + k, 1), :], (8, LANES)) for k in range(2)] for t in range(tiles)
    ]


def step_row(src, coef, row, group, masks, ring, last):
    tiles = len(masks) - 1
    s = pl.ds(group * 8, 8)
    lane = lax.broadcasted_iota(jnp.int32, (8, LANES), 1)
    here = [src[row, t, s, :] for t in range(tiles + 1)]
    if ring is None:
        low, high = here[tiles], here[tiles]
    else:
        low, high = ring[0][row - 1, s, :], ring[1][row - 1, s, :]
    fwd = [pltpu.roll(h, NZ, 1) for h in here[:tiles] + [low]]
    bwd = [pltpu.roll(h, LANES - NZ, 1) for h in here[:tiles] + [high]]
    own = (fwd[tiles], bwd[tiles])
    if ring is not None:
        half = lane < LANES // 2
        own = (
            jnp.where(half, pltpu.roll(high, NZ, 1), fwd[tiles]),
            jnp.where(half, bwd[tiles], pltpu.roll(low, LANES - NZ, 1)),
        )
    one = [pltpu.roll(h, 1, 1) for h in here]
    neg = [pltpu.roll(h, LANES - 1, 1) for h in here]
    new = []
    for t in range(tiles if last else tiles + 1):
        before, after = (t - 1) % (tiles + 1), (t + 1) % (tiles + 1)
        mine = own if t == tiles else (fwd[t], bwd[t])
        beside = (src[row - 1, t, s, :] + src[row + 1, t, s, :]) + (
            jnp.where(lane < NZ, fwd[before], mine[0]) + jnp.where(lane >= LANES - NZ, bwd[after], mine[1])
        )
        starts = (t * LANES) % NZ == 0
        stops = ((t + 1) * LANES) % NZ == 0
        below = one[t] if starts else jnp.where(lane < 1, one[before], one[t])
        above = neg[t] if stops else jnp.where(lane >= LANES - 1, neg[after], neg[t])
        beside = beside + (masks[t][0] * below + masks[t][1] * above)
        new.append(coef[t][1] * here[t] + coef[t][0] * beside)
    return new


def step_kernel(batch, e0_in, xu_in, hxa, hxb, hya, hyb, ca, cb, s_gram, out, e0, xu, e1, e2, low, high):
    cols = xu.shape[0]
    tiles = e0.shape[1] - 1
    count = xu.shape[1] // 2 - ROWS
    base = 2 * count
    odd_x = lax.rem(lax.axis_index("gx"), 2) == 1
    odd_y = lax.rem(lax.axis_index("gy"), 2) == 1
    lane = lax.broadcasted_iota(jnp.int32, (ROWS, LANES), 1)
    e0[0, tiles] = jnp.zeros((ROWS, LANES), F32)
    e0[cols + 2 * STEPS - 1, tiles] = jnp.zeros((ROWS, LANES), F32)

    def place_x(up, down):
        e0[0:STEPS, 0:tiles] = up[...]
        e0[cols + STEPS :, 0:tiles] = down[...]

    def place_y(lo, hi, lo_ends, hi_ends):
        for r in range(cols + 4):
            k = r - 2
            inside = 0 <= k < cols
            end = r if k < 0 else r - cols
            lo_row = lo[k] if inside else lo_ends[end]
            hi_row = hi[k] if inside else hi_ends[end]
            low[r] = lo_row
            high[r] = hi_row
            e0[r + 1, tiles] = jnp.where(lane < LANES // 2, hi_row, lo_row)

    pl.when(odd_x)(lambda: place_x(hxa, hxb))
    pl.when(jnp.logical_not(odd_x))(lambda: place_x(hxb, hxa))
    pl.when(odd_y)(lambda: place_y(hya, hyb, ca, cb))
    pl.when(jnp.logical_not(odd_y))(lambda: place_y(hyb, hya, cb, ca))
    masks = z_masks(tiles)

    def sweep(src, dst, start, stop, ring):
        unroll = max(u for u in range(1, UNROLL + 1) if (stop - start) % u == 0)

        @pl.loop(0, (stop - start) // unroll)
        def _(k):
            for j in range(unroll):
                row = start + k * unroll + j
                coef = row_coef(e0, row, batch, tiles + 1)
                for group in range(ROWS // 8):
                    for t, v in enumerate(step_row(src, coef, row, group, masks, ring, False)):
                        dst[row, t, pl.ds(group * 8, 8), :] = v

    sweep(e0, e1, 1, cols + 5, (low, high))
    sweep(e1, e2, 2, cols + 4, None)

    @pl.loop(0, cols // 4)
    def _(k):
        for j in range(4):
            i = k * 4 + j
            coef = row_coef(e0, i + STEPS, batch, tiles)
            for pair in range(ROWS // 16):
                parts = [step_row(e2, coef, i + STEPS, 2 * pair + k, masks, None, True) for k in range(2)]
                for t in range(tiles):
                    h, l = split(jnp.concatenate([parts[0][t], parts[1][t]], 0))
                    xu[i, pl.ds(base + pair * 16, 16), t * LANES : (t + 1) * LANES] = h
                    xu[i, pl.ds(base + ROWS + pair * 16, 16), t * LANES : (t + 1) * LANES] = l

    acc = None
    for i in range(cols):
        part = dot_t(xu[i], xu[i, base:, :])
        acc = part if acc is None else acc + part
    u = acc[0:count, :] + acc[count:base, :]
    x = acc[base : base + ROWS, :] + acc[base + ROWS :, :]
    u = u[:, 0:ROWS] + u[:, ROWS:]
    s = s_gram[...]
    half = count // 2
    quarter = half // 2
    x = x[:, 0:ROWS] + x[:, ROWS:]
    out[0:half, :] = jnp.concatenate([u[0:half], u[half:], x, s[0:half, half:]], 1)
    corner = [s[k * half : (k + 1) * half, k * half : (k + 1) * half] for k in range(2)]
    out[half:, :] = jnp.concatenate([c[k * quarter : (k + 1) * quarter] for c in corner for k in range(2)], 1)


def last_kernel(batch, cells, total, sigma, xu, basis, core, buf, sem):
    cols = xu.shape[0]
    count = xu.shape[1] // 2 - ROWS
    half = count // 2
    inverse = 1.0 / cells
    blocks = [total[0:half, k * half : (k + 1) * half] for k in range(4)]
    pieces = [total[half:, k * half : (k + 1) * half] for k in range(4)]
    col = lax.broadcasted_iota(jnp.int32, (count, ROWS), 1)
    c = jnp.where(col < batch, jnp.concatenate(blocks[:2], 0), 0.0)
    rows = lax.broadcasted_iota(jnp.int32, (ROWS, ROWS), 0)
    lanes = lax.broadcasted_iota(jnp.int32, (ROWS, ROWS), 1)
    g = blocks[2]
    s = jnp.concatenate(
        [
            jnp.concatenate([jnp.concatenate(pieces[:2], 0), blocks[3]], 1),
            jnp.concatenate([blocks[3].T, jnp.concatenate(pieces[2:], 0)], 1),
        ],
        0,
    )
    first = c * inverse
    both = first + (c - small_dot(s, first)) * inverse
    rest = small_dot(s, both) - c
    gram = g - small_dot(c, both, ((0,), (0,))) + small_dot(both, rest, ((0,), (0,)))
    gram = jnp.where((rows < batch) & (lanes < batch), gram * inverse, jnp.where(rows == lanes, 1.0, 0.0))
    m = jnp.concatenate([gram, jnp.where(rows == lanes, 1.0, 0.0)], 1)
    index = lax.broadcasted_iota(jnp.int32, (8, LANES), 0)
    groups = ROWS // 8
    m = jnp.concatenate([m, jnp.zeros((ROWS, LANES - 2 * ROWS), F32)], 1)
    m = [m[8 * q : 8 * q + 8] for q in range(groups)]
    columns = [[jnp.broadcast_to(m[q][:, j : j + 1], (8, LANES)) for q in range(groups)] for j in range(batch)]
    for j in range(batch):
        at, row = j // 8, j % 8
        pivot = columns[j][at][row : row + 1]
        factor = {}
        for q in range(at, groups):
            value = columns[j][q] * (1.0 / pivot)
            factor[q] = jnp.where(index > row, value, 0.0) if q == at else value
        for k in range(j + 1, batch):
            top = columns[k][at][row : row + 1]
            for q in range(at, groups):
                columns[k][q] = columns[k][q] - factor[q] * top
        top = m[at][row : row + 1]
        for q in range(at, groups):
            m[q] = m[q] - factor[q] * top
        m[at] = jnp.where(index == row, m[at] * lax.rsqrt(pivot), m[at])
    m = jnp.concatenate(m, 0)
    upper = jnp.where(rows <= lanes, m[:, 0:ROWS], 0.0)
    linv = m[:, ROWS : 2 * ROWS]
    wu = -small_dot(linv, both, ((1,), (1,)))
    xh, xl = split(linv)
    uh, ul = split(wu)
    w = jnp.concatenate(
        [jnp.concatenate([uh, uh, xh, xh], 1), jnp.concatenate([ul, ul, xl, xl], 1)], 0
    )
    copies = [pltpu.make_async_copy(buf.at[i], basis.at[:, i, :], sem.at[i]) for i in range(cols)]
    for start in range(0, cols, GROUP):
        for i in range(start, start + GROUP):
            value = jnp.dot(w, xu[i], preferred_element_type=F32)
            buf[i] = value[0:batch] + value[ROWS : ROWS + batch]
        for i in range(start, start + GROUP):
            copies[i].start()
    core[...] = jnp.zeros_like(core)
    er = lax.broadcasted_iota(jnp.int32, (count, count), 0)
    ec = lax.broadcasted_iota(jnp.int32, (count, count), 1)
    core[0:count, 0:count] = jnp.where(er == ec, sigma[...], 0.0)
    core[0:count, count:] = both[:, 0:batch]
    core[count:, count:] = upper[0:batch, 0:batch]
    for copy in copies:
        copy.wait()


def in_hbm(value):
    return pltpu.with_memory_space_constraint(value, pltpu.HBM)


def swap(value, axis, offset):
    count = lax.axis_size(axis)
    pairs = [(i, i + 1) for i in range(offset, count - 1, 2)]
    return lax.ppermute(value, axis, pairs + [(j, i) for i, j in pairs])


def exchanged_sum(value, axis, offsets):
    count = lax.axis_size(axis)
    terms = [value] + [lax.ppermute(value, axis, [(i, i ^ k) for i in range(count)]) for k in offsets]
    while len(terms) > 1:
        terms = [a + b for a, b in zip(terms[::2], terms[1::2])]
    return terms[0]


def total_sum(value):
    for axis in ("gy", "gx"):
        count = lax.axis_size(axis)
        if count & (count - 1):
            value = lax.psum(value, axis)
            continue
        step = 1
        while step < count:
            odd = (count // step).bit_length() % 2 == 0
            value = exchanged_sum(value, axis, [step] if odd else [step, 2 * step, 3 * step])
            step *= 2 if odd else 4
    return value


def body(snapshots, modes, mobility, phase, contact, sigma):
    batch, cols, width = snapshots.shape
    count = modes.shape[0]
    tiles = width // LANES
    vmem = pl.BlockSpec(memory_space=pltpu.VMEM)
    hbm = pl.BlockSpec(memory_space=pltpu.HBM)
    shape = jax.ShapeDtypeStruct
    params = pltpu.CompilerParams(vmem_limit_bytes=40 << 20)
    coef, sxa, sxb, sya, syb = pl.pallas_call(
        edge_kernel,
        out_shape=(shape((2, cols, width), F32),)
        + (shape((STEPS, tiles, ROWS, LANES), F32),) * 2
        + (shape((cols, ROWS, LANES), F32),) * 2,
        in_specs=[hbm] * 4,
        out_specs=(vmem,) * 5,
        scratch_shapes=[
            pltpu.VMEM((2 * STEPS, batch, width), F32),
            pltpu.VMEM((cols - 2 * STEPS, 2, batch, LANES), F32),
            pltpu.VMEM((cols, width), F32),
            pltpu.VMEM((cols, width), jnp.int32),
            pltpu.VMEM((cols, width), jnp.int32),
            pltpu.VMEM((2 * STEPS, tiles, ROWS, LANES), F32),
            pltpu.VMEM((2, cols, ROWS, LANES), F32),
            pltpu.SemaphoreType.DMA((2 * cols - 2 * STEPS,)),
            pltpu.SemaphoreType.DMA((3,)),
        ],
        compiler_params=params,
        name="edge",
    )(*(in_hbm(v) for v in (snapshots, mobility, phase, contact)))
    odd_x = lax.axis_index("gx") % 2 == 1
    odd_y = lax.axis_index("gy") % 2 == 1
    hxa = swap(sxa, "gx", 0)
    hxb = swap(sxb, "gx", 1)
    hya = swap(sya, "gy", 0)
    hyb = swap(syb, "gy", 1)
    ext = (cols + 2 * STEPS, tiles + 1, ROWS, LANES)
    xu, s_gram, e0 = pl.pallas_call(
        modes_kernel,
        out_shape=(shape((cols, 2 * (count + ROWS), width), BF16), shape((count, count), F32), shape(ext, F32)),
        in_specs=[hbm, hbm, vmem],
        out_specs=(vmem,) * 3,
        scratch_shapes=[
            pltpu.VMEM((cols, count, width), F32),
            pltpu.VMEM((cols, batch, width), F32),
            pltpu.SemaphoreType.DMA((2 * cols,)),
        ],
        compiler_params=params,
        cost_estimate=pl.CostEstimate(flops=2 * cols * width * 4 * count * count, bytes_accessed=8 * cols * width * count, transcendentals=0),
        name="modes",
    )(in_hbm(modes), in_hbm(snapshots), coef)
    hxa, hxb, s_gram = lax.optimization_barrier((hxa, hxb, s_gram))

    def corners(low_side):
        side = [jnp.where(low_side, h[:, 0], h[:, tiles - 1]) for h in (hxa, hxb)]
        up = jnp.where(odd_x, side[0][1:], side[1][1:])
        down = jnp.where(odd_x, side[1][:2], side[0][:2])
        return jnp.concatenate([up, down], 0)

    ca = swap(corners(odd_y), "gy", 0)
    cb = swap(corners(jnp.logical_not(odd_y)), "gy", 1)
    halo = pltpu.VMEM((cols + 4, ROWS, LANES), F32)
    part, _, xu = pl.pallas_call(
        lambda *refs: step_kernel(batch, *refs),
        out_shape=(
            shape((3 * count // 4, 2 * count), F32),
            shape(ext, F32),
            shape((cols, 2 * (count + ROWS), width), BF16),
        ),
        in_specs=[vmem] * 9,
        out_specs=(vmem,) * 3,
        scratch_shapes=[
            pltpu.VMEM(ext, F32),
            pltpu.VMEM(ext, F32),
            halo,
            halo,
        ],
        input_output_aliases={0: 1, 1: 2},
        compiler_params=params,
        name="steps",
    )(e0, xu, hxa, hxb, hya, hyb, ca, cb, s_gram)
    total = total_sum(part)
    cells = float(cols * width * lax.axis_size("gx") * lax.axis_size("gy"))
    basis, core = pl.pallas_call(
        lambda *refs: last_kernel(batch, cells, *refs),
        out_shape=(shape(snapshots.shape, F32), shape((count + batch, count + batch), F32)),
        in_specs=[vmem] * 3,
        out_specs=(hbm, vmem),
        scratch_shapes=[pltpu.VMEM((cols, batch, width), F32), pltpu.SemaphoreType.DMA((cols,))],
        compiler_params=params,
        name="last",
    )(total, sigma.reshape(1, count), xu)
    return (basis, core)


def solution(mesh):
    return jax.shard_map(
        body,
        mesh=mesh,
        in_specs=(
            P(None, "gx", "gy"),
            P(None, "gx", "gy"),
            P("gx", "gy"),
            P("gx", "gy"),
            P("gx", "gy"),
            P(),
        ),
        out_specs=(P(None, "gx", "gy"), P()),
        check_vma=False,
    )
```

```python
import jax
import jax.numpy as jnp
from jax import lax
from jax.experimental import pallas as pl
from jax.experimental.pallas import tpu as pltpu
from jax.sharding import PartitionSpec as P

NZ = 24
STEPS = 3
LANES = 128
ROWS = 32
UNROLL = 7
GROUP = 8
HIGH = lax.Precision.HIGHEST
F32 = jnp.float32
BF16 = jnp.bfloat16


def split(value):
    high = value.astype(BF16)
    return high, (value - high.astype(F32)).astype(BF16)


def dot_t(a, b):
    return lax.dot_general(a, b, (((1,), (1,)), ((), ())), preferred_element_type=F32)


def small_dot(a, b, dims=((1,), (0,))):
    return lax.dot_general(a, b, (dims, ((), ())), precision=HIGH, preferred_element_type=F32)


def fill_rows(dst, index, fields, rate, keep):
    batch = fields.shape[0]
    dst[index + (pl.ds(0, batch),)] = fields
    dst[index + (pl.ds(batch, 1),)] = rate
    dst[index + (pl.ds(batch + 1, 1),)] = keep
    dst[index + (pl.ds(batch + 2, ROWS - batch - 2),)] = jnp.zeros((ROWS - batch - 2, LANES), F32)


def pack_spots(cols):
    span = STEPS * NZ
    return [(r, r * span // LANES, r * span % LANES) for r in range(cols)]


def packed_tiles(cols):
    return pl.cdiv(cols * STEPS * NZ, LANES)


def edge_kernel(snap, mob, pha, con, coef, sxa, sxb, sya, syb, bufx, bufy, vm, vp, vc, rows, cols_y, packed, sem, sem_c):
    batch, cols, width = snap.shape
    tiles = width // LANES
    small = [
        pltpu.make_async_copy(ref, dst, sem_c.at[i])
        for i, (ref, dst) in enumerate(((mob, vm), (pha, vp), (con, vc)))
    ]
    outer = list(range(STEPS)) + list(range(cols - STEPS, cols))
    inner = list(range(STEPS, cols - STEPS))
    copies = [pltpu.make_async_copy(snap.at[:, i, :], bufx.at[k], sem.at[k]) for k, i in enumerate(outer)]
    for k, i in enumerate(inner):
        for side, start in enumerate((0, width - LANES)):
            n = len(outer) + 2 * k + side
            copies.append(
                pltpu.make_async_copy(snap.at[:, i, pl.ds(start, LANES)], bufy.at[k, side], sem.at[n])
            )
    for copy in small + copies:
        copy.start()
    for copy in small:
        copy.wait()
    rate = vm[...] * jnp.where(vp[...] == 1, 1.0, 0.5).astype(F32)
    lane = lax.broadcasted_iota(jnp.int32, (cols, width), 1) % NZ
    ends = jnp.where(lane == 0, 1.0, 0.0) + jnp.where(lane == NZ - 1, 1.0, 0.0)
    keep = 1.0 - 0.25 * vc[...].astype(F32) - rate * (6.0 - ends)
    coef[0] = rate
    coef[1] = keep
    for k, i in enumerate(outer):
        copies[k].wait()
        for t in range(tiles):
            span = slice(t * LANES, (t + 1) * LANES)
            fill_rows(rows, (k, t), bufx[k, :, span], rate[i : i + 1, span], keep[i : i + 1, span])
        for side, t in enumerate((0, tiles - 1)):
            cols_y[side, i] = rows[k, t]
    for k, i in enumerate(inner):
        for side, t in enumerate((0, tiles - 1)):
            copies[len(outer) + 2 * k + side].wait()
            span = slice(t * LANES, (t + 1) * LANES)
            fill_rows(cols_y, (side, i), bufy[k, side], rate[i : i + 1, span], keep[i : i + 1, span])
    odd_x = lax.rem(lax.axis_index("gx"), 2)
    odd_y = lax.rem(lax.axis_index("gy"), 2)
    sxa[...] = rows[pl.ds((1 - odd_x) * STEPS, STEPS)]
    sxb[...] = rows[pl.ds(odd_x * STEPS, STEPS)]
    wide = lax.broadcasted_iota(jnp.int32, (ROWS, LANES), 1)
    span = STEPS * NZ
    for side in range(2):
        tail = None
        for r, tile, spot in pack_spots(cols):
            value = pltpu.roll(cols_y[side, r], (spot + side * span) % LANES, 1)
            packed[side, tile] = value if spot == 0 else jnp.where(wide >= spot, value, tail)
            if spot + span < LANES:
                tail = packed[side, tile]
            else:
                tail = value
                if tile + 1 < packed.shape[1]:
                    packed[side, tile + 1] = value
    sya[...] = packed[1 - odd_y]
    syb[...] = packed[odd_y]


def modes_kernel(modes, snap, coef, xu, gram, e0, buf, bufx, sem):
    count, cols, width = modes.shape
    batch = snap.shape[0]
    copies = [pltpu.make_async_copy(snap.at[:, i, :], bufx.at[i], sem.at[i]) for i in range(cols)]
    copies += [pltpu.make_async_copy(modes.at[:, i, :], buf.at[i], sem.at[cols + i]) for i in range(cols)]
    for copy in copies:
        copy.start()
    for i in range(cols):
        copies[i].wait()
        for t in range(width // LANES):
            span = slice(t * LANES, (t + 1) * LANES)
            fill_rows(e0, (i + STEPS, t), bufx[i, :, span], coef[0, i : i + 1, span], coef[1, i : i + 1, span])
    for i in range(cols):
        copies[cols + i].wait()
        high, low = split(buf[i])
        xu[i, 0:count, :] = high
        xu[i, count : 2 * count, :] = low
    acc = None
    for i in range(cols):
        part = dot_t(xu[i, 0 : 2 * count, :], xu[i, 0:count, :])
        acc = part if acc is None else acc + part
    cross = acc[count : 2 * count]
    gram[...] = acc[0:count] + (cross + cross.T)


def z_masks(tiles):
    lane = lax.broadcasted_iota(jnp.int32, (8, LANES), 1)
    found = []
    for t in range(tiles + 1):
        z = (lane + t * LANES) % NZ if t < tiles else jnp.where(lane < LANES // 2, lane % NZ, (lane + 16) % NZ)
        found.append((jnp.where(z == 0, 0.0, 1.0), jnp.where(z == NZ - 1, 0.0, 1.0)))
    return found


def row_coef(base, row, batch, tiles):
    return [
        [jnp.broadcast_to(base[row, t, pl.ds(batch + k, 1), :], (8, LANES)) for k in range(2)] for t in range(tiles)
    ]


def step_row(src, coef, row, group, masks, ring, last):
    tiles = len(masks) - 1
    s = pl.ds(group * 8, 8)
    lane = lax.broadcasted_iota(jnp.int32, (8, LANES), 1)
    here = [src[row, t, s, :] for t in range(tiles + 1)]
    if ring is None:
        low, high = here[tiles], here[tiles]
    else:
        low, high = ring[0][row - 1, s, :], ring[1][row - 1, s, :]
    fwd = [pltpu.roll(h, NZ, 1) for h in here[:tiles] + [low]]
    bwd = [pltpu.roll(h, LANES - NZ, 1) for h in here[:tiles] + [high]]
    own = (fwd[tiles], bwd[tiles])
    if ring is not None:
        half = lane < LANES // 2
        own = (
            jnp.where(half, pltpu.roll(high, NZ, 1), fwd[tiles]),
            jnp.where(half, bwd[tiles], pltpu.roll(low, LANES - NZ, 1)),
        )
    one = [pltpu.roll(h, 1, 1) for h in here]
    neg = [pltpu.roll(h, LANES - 1, 1) for h in here]
    new = []
    for t in range(tiles if last else tiles + 1):
        before, after = (t - 1) % (tiles + 1), (t + 1) % (tiles + 1)
        mine = own if t == tiles else (fwd[t], bwd[t])
        beside = (src[row - 1, t, s, :] + src[row + 1, t, s, :]) + (
            jnp.where(lane < NZ, fwd[before], mine[0]) + jnp.where(lane >= LANES - NZ, bwd[after], mine[1])
        )
        starts = (t * LANES) % NZ == 0
        stops = ((t + 1) * LANES) % NZ == 0
        below = one[t] if starts else jnp.where(lane < 1, one[before], one[t])
        above = neg[t] if stops else jnp.where(lane >= LANES - 1, neg[after], neg[t])
        beside = beside + (masks[t][0] * below + masks[t][1] * above)
        new.append(coef[t][1] * here[t] + coef[t][0] * beside)
    return new


def place_sides(e0, low, high, sides, ends, rows):
    cols = e0.shape[0] - 2 * STEPS
    tiles = e0.shape[1] - 1
    span = STEPS * NZ
    spots = pack_spots(cols)
    lane = lax.broadcasted_iota(jnp.int32, (ROWS, LANES), 1)

    def place(lo, hi, lo_ends, hi_ends):
        for r in rows:
            k = r - 2
            if 0 <= k < cols:
                _, tile, spot = spots[k]
                lo_row, hi_row = lo[tile], hi[tile]
                if spot + span > LANES:
                    lo_row = jnp.where(lane >= spot, lo_row, lo[tile + 1])
                    hi_row = jnp.where(lane >= spot, hi_row, hi[tile + 1])
                lo_row = pltpu.roll(lo_row, (2 * LANES - span - spot) % LANES, 1)
                hi_row = pltpu.roll(hi_row, (LANES - spot) % LANES, 1)
            else:
                end = r if k < 0 else r - cols
                lo_row, hi_row = lo_ends[end], hi_ends[end]
            low[r] = lo_row
            high[r] = hi_row
            e0[r + 1, tiles] = jnp.where(lane < LANES // 2, hi_row, lo_row)

    odd_y = lax.rem(lax.axis_index("gy"), 2) == 1
    pl.when(odd_y)(lambda: place(sides[0], sides[1], ends[0], ends[1]))
    pl.when(jnp.logical_not(odd_y))(lambda: place(sides[1], sides[0], ends[1], ends[0]))


def sweep(src, dst, base, start, stop, batch, masks, ring):
    tiles = len(masks)
    unroll = max(u for u in range(1, UNROLL + 1) if (stop - start) % u == 0)

    @pl.loop(0, (stop - start) // unroll)
    def _(k):
        for j in range(unroll):
            row = start + k * unroll + j
            coef = row_coef(base, row, batch, tiles)
            for group in range(ROWS // 8):
                for t, v in enumerate(step_row(src, coef, row, group, masks, ring, False)):
                    dst[row, t, pl.ds(group * 8, 8), :] = v


def final_sweep(src, xu, base, start, stop, batch, masks):
    tiles = len(masks) - 1
    first = xu.shape[1] - 2 * ROWS
    unroll = max(u for u in range(1, UNROLL + 1) if (stop - start) % u == 0)

    @pl.loop(0, (stop - start) // unroll)
    def _(k):
        for j in range(unroll):
            i = start + k * unroll + j
            coef = row_coef(base, i + STEPS, batch, tiles)
            for pair in range(ROWS // 16):
                parts = [step_row(src, coef, i + STEPS, 2 * pair + h, masks, None, True) for h in range(2)]
                for t in range(tiles):
                    h, l = split(jnp.concatenate([parts[0][t], parts[1][t]], 0))
                    xu[i, pl.ds(first + pair * 16, 16), t * LANES : (t + 1) * LANES] = h
                    xu[i, pl.ds(first + ROWS + pair * 16, 16), t * LANES : (t + 1) * LANES] = l


def products(xu, rows, acc):
    first = xu.shape[1] - 2 * ROWS
    for i in rows:
        part = dot_t(xu[i], xu[i, first:, :])
        acc = part if acc is None else acc + part
    return acc


def inner_kernel(batch, e0_in, xu_in, hya, hyb, acc, e0, xu, e1, e2, low, high):
    cols = xu.shape[0]
    masks = z_masks(e0.shape[1] - 1)
    place_sides(e0, low, high, (hya, hyb), (None, None), range(2, cols + 2))
    sweep(e0, e1, e0, STEPS + 1, cols + STEPS - 1, batch, masks, (low, high))
    sweep(e1, e2, e0, STEPS + 2, cols + STEPS - 2, batch, masks, None)
    final_sweep(e2, xu, e0, STEPS, cols - STEPS, batch, masks)
    acc[...] = products(xu, range(STEPS, cols - STEPS), None)


def outer_kernel(batch, e0_in, xu_in, e1_in, e2_in, hxa, hxb, hya, hyb, ca, cb, acc_in, s_gram, out, e0, xu, e1, e2, low, high):
    cols = xu.shape[0]
    tiles = e0.shape[1] - 1
    base = xu.shape[1] - 2 * ROWS
    count = base // 2
    odd_x = lax.rem(lax.axis_index("gx"), 2) == 1
    e0[0, tiles] = jnp.zeros((ROWS, LANES), F32)
    e0[cols + 2 * STEPS - 1, tiles] = jnp.zeros((ROWS, LANES), F32)

    def place_x(up, down):
        e0[0:STEPS, 0:tiles] = up[...]
        e0[cols + STEPS :, 0:tiles] = down[...]

    pl.when(odd_x)(lambda: place_x(hxa, hxb))
    pl.when(jnp.logical_not(odd_x))(lambda: place_x(hxb, hxa))
    place_sides(e0, low, high, (hya, hyb), (ca, cb), (0, 1, 2, cols + 1, cols + 2, cols + 3))
    masks = z_masks(tiles)
    sweep(e0, e1, e0, 1, STEPS + 1, batch, masks, (low, high))
    sweep(e0, e1, e0, cols + STEPS - 1, cols + 5, batch, masks, (low, high))
    sweep(e1, e2, e0, 2, STEPS + 2, batch, masks, None)
    sweep(e1, e2, e0, cols + STEPS - 2, cols + 4, batch, masks, None)
    final_sweep(e2, xu, e0, 0, STEPS, batch, masks)
    final_sweep(e2, xu, e0, cols - STEPS, cols, batch, masks)
    acc = products(xu, list(range(STEPS)) + list(range(cols - STEPS, cols)), acc_in[...])
    u = acc[0:count, :] + acc[count:base, :]
    x = acc[base : base + ROWS, :] + acc[base + ROWS :, :]
    u = u[:, 0:ROWS] + u[:, ROWS:]
    s = s_gram[...]
    half = count // 2
    quarter = half // 2
    x = x[:, 0:ROWS] + x[:, ROWS:]
    out[0:half, :] = jnp.concatenate([u[0:half], u[half:], x, s[0:half, half:]], 1)
    corner = [s[k * half : (k + 1) * half, k * half : (k + 1) * half] for k in range(2)]
    out[half:, :] = jnp.concatenate([c[k * quarter : (k + 1) * quarter] for c in corner for k in range(2)], 1)


def last_kernel(batch, cells, total, sigma, xu, basis, core, buf, sem):
    cols = xu.shape[0]
    count = xu.shape[1] // 2 - ROWS
    half = count // 2
    inverse = 1.0 / cells
    blocks = [total[0:half, k * half : (k + 1) * half] for k in range(4)]
    pieces = [total[half:, k * half : (k + 1) * half] for k in range(4)]
    col = lax.broadcasted_iota(jnp.int32, (count, ROWS), 1)
    c = jnp.where(col < batch, jnp.concatenate(blocks[:2], 0), 0.0)
    rows = lax.broadcasted_iota(jnp.int32, (ROWS, ROWS), 0)
    lanes = lax.broadcasted_iota(jnp.int32, (ROWS, ROWS), 1)
    g = blocks[2]
    s = jnp.concatenate(
        [
            jnp.concatenate([jnp.concatenate(pieces[:2], 0), blocks[3]], 1),
            jnp.concatenate([blocks[3].T, jnp.concatenate(pieces[2:], 0)], 1),
        ],
        0,
    )
    first = c * inverse
    both = first + (c - small_dot(s, first)) * inverse
    rest = small_dot(s, both) - c
    gram = g - small_dot(c, both, ((0,), (0,))) + small_dot(both, rest, ((0,), (0,)))
    gram = jnp.where((rows < batch) & (lanes < batch), gram * inverse, jnp.where(rows == lanes, 1.0, 0.0))
    m = jnp.concatenate([gram, jnp.where(rows == lanes, 1.0, 0.0)], 1)
    index = lax.broadcasted_iota(jnp.int32, (8, LANES), 0)
    groups = ROWS // 8
    m = jnp.concatenate([m, jnp.zeros((ROWS, LANES - 2 * ROWS), F32)], 1)
    m = [m[8 * q : 8 * q + 8] for q in range(groups)]
    columns = [[jnp.broadcast_to(m[q][:, j : j + 1], (8, LANES)) for q in range(groups)] for j in range(batch)]
    for j in range(batch):
        at, row = j // 8, j % 8
        pivot = columns[j][at][row : row + 1]
        factor = {}
        for q in range(at, groups):
            value = columns[j][q] * (1.0 / pivot)
            factor[q] = jnp.where(index > row, value, 0.0) if q == at else value
        for k in range(j + 1, batch):
            top = columns[k][at][row : row + 1]
            for q in range(at, groups):
                columns[k][q] = columns[k][q] - factor[q] * top
        top = m[at][row : row + 1]
        for q in range(at, groups):
            m[q] = m[q] - factor[q] * top
        m[at] = jnp.where(index == row, m[at] * lax.rsqrt(pivot), m[at])
    m = jnp.concatenate(m, 0)
    upper = jnp.where(rows <= lanes, m[:, 0:ROWS], 0.0)
    linv = m[:, ROWS : 2 * ROWS]
    wu = -small_dot(linv, both, ((1,), (1,)))
    xh, xl = split(linv)
    uh, ul = split(wu)
    w = jnp.concatenate(
        [jnp.concatenate([uh, uh, xh, xh], 1), jnp.concatenate([ul, ul, xl, xl], 1)], 0
    )
    copies = [pltpu.make_async_copy(buf.at[i], basis.at[:, i, :], sem.at[i]) for i in range(cols)]
    for start in range(0, cols, GROUP):
        for i in range(start, start + GROUP):
            value = jnp.dot(w, xu[i], preferred_element_type=F32)
            buf[i] = value[0:batch] + value[ROWS : ROWS + batch]
        for i in range(start, start + GROUP):
            copies[i].start()
    core[...] = jnp.zeros_like(core)
    er = lax.broadcasted_iota(jnp.int32, (count, count), 0)
    ec = lax.broadcasted_iota(jnp.int32, (count, count), 1)
    core[0:count, 0:count] = jnp.where(er == ec, sigma[...], 0.0)
    core[0:count, count:] = both[:, 0:batch]
    core[count:, count:] = upper[0:batch, 0:batch]
    for copy in copies:
        copy.wait()


def in_hbm(value):
    return pltpu.with_memory_space_constraint(value, pltpu.HBM)


def swap(value, axis, offset):
    count = lax.axis_size(axis)
    pairs = [(i, i + 1) for i in range(offset, count - 1, 2)]
    return lax.ppermute(value, axis, pairs + [(j, i) for i, j in pairs])


def exchanged_sum(value, axis, offsets):
    count = lax.axis_size(axis)
    terms = [value] + [lax.ppermute(value, axis, [(i, i ^ k) for i in range(count)]) for k in offsets]
    while len(terms) > 1:
        terms = [a + b for a, b in zip(terms[::2], terms[1::2])]
    return terms[0]


def total_sum(value):
    for axis in ("gy", "gx"):
        count = lax.axis_size(axis)
        if count & (count - 1):
            value = lax.psum(value, axis)
            continue
        step = 1
        while step < count:
            odd = (count // step).bit_length() % 2 == 0
            value = exchanged_sum(value, axis, [step] if odd else [step, 2 * step, 3 * step])
            step *= 2 if odd else 4
    return value


def body(snapshots, modes, mobility, phase, contact, sigma):
    batch, cols, width = snapshots.shape
    count = modes.shape[0]
    tiles = width // LANES
    vmem = pl.BlockSpec(memory_space=pltpu.VMEM)
    hbm = pl.BlockSpec(memory_space=pltpu.HBM)
    shape = jax.ShapeDtypeStruct
    params = pltpu.CompilerParams(vmem_limit_bytes=40 << 20)
    coef, sxa, sxb, sya, syb = pl.pallas_call(
        edge_kernel,
        out_shape=(shape((2, cols, width), F32),)
        + (shape((STEPS, tiles, ROWS, LANES), F32),) * 2
        + (shape((packed_tiles(cols), ROWS, LANES), F32),) * 2,
        in_specs=[hbm] * 4,
        out_specs=(vmem,) * 5,
        scratch_shapes=[
            pltpu.VMEM((2 * STEPS, batch, width), F32),
            pltpu.VMEM((cols - 2 * STEPS, 2, batch, LANES), F32),
            pltpu.VMEM((cols, width), F32),
            pltpu.VMEM((cols, width), jnp.int32),
            pltpu.VMEM((cols, width), jnp.int32),
            pltpu.VMEM((2 * STEPS, tiles, ROWS, LANES), F32),
            pltpu.VMEM((2, cols, ROWS, LANES), F32),
            pltpu.VMEM((2, packed_tiles(cols), ROWS, LANES), F32),
            pltpu.SemaphoreType.DMA((2 * cols - 2 * STEPS,)),
            pltpu.SemaphoreType.DMA((3,)),
        ],
        compiler_params=params,
        name="edge",
    )(*(in_hbm(v) for v in (snapshots, mobility, phase, contact)))
    odd_x = lax.axis_index("gx") % 2 == 1
    odd_y = lax.axis_index("gy") % 2 == 1
    hxa = swap(sxa, "gx", 0)
    hxb = swap(sxb, "gx", 1)
    hya = swap(sya, "gy", 0)
    hyb = swap(syb, "gy", 1)
    ext = (cols + 2 * STEPS, tiles + 1, ROWS, LANES)
    xu, s_gram, e0 = pl.pallas_call(
        modes_kernel,
        out_shape=(shape((cols, 2 * (count + ROWS), width), BF16), shape((count, count), F32), shape(ext, F32)),
        in_specs=[hbm, hbm, vmem],
        out_specs=(vmem,) * 3,
        scratch_shapes=[
            pltpu.VMEM((cols, count, width), F32),
            pltpu.VMEM((cols, batch, width), F32),
            pltpu.SemaphoreType.DMA((2 * cols,)),
        ],
        compiler_params=params,
        cost_estimate=pl.CostEstimate(flops=2 * cols * width * 4 * count * count, bytes_accessed=8 * cols * width * count, transcendentals=0),
        name="modes",
    )(in_hbm(modes), in_hbm(snapshots), coef)
    hxa, hxb, s_gram = lax.optimization_barrier((hxa, hxb, s_gram))

    def corners(low_side):
        side = [jnp.where(low_side, h[:, 0], h[:, tiles - 1]) for h in (hxa, hxb)]
        up = jnp.where(odd_x, side[0][1:], side[1][1:])
        down = jnp.where(odd_x, side[1][:2], side[0][:2])
        return jnp.concatenate([up, down], 0)

    ca = swap(corners(odd_y), "gy", 0)
    cb = swap(corners(jnp.logical_not(odd_y)), "gy", 1)
    halo = pltpu.VMEM((cols + 4, ROWS, LANES), F32)
    fields = shape(ext, F32)
    both = shape((cols, 2 * (count + ROWS), width), BF16)
    acc, e0, xu, e1, e2 = pl.pallas_call(
        lambda *refs: inner_kernel(batch, *refs),
        out_shape=(shape((2 * (count + ROWS), 2 * ROWS), F32), fields, both, fields, fields),
        in_specs=[vmem] * 4,
        out_specs=(vmem,) * 5,
        scratch_shapes=[halo, halo],
        input_output_aliases={0: 1, 1: 2},
        compiler_params=params,
        cost_estimate=pl.CostEstimate(flops=40 * cols * width * ROWS, bytes_accessed=8 * cols * width * count, transcendentals=0),
        name="inner",
    )(e0, xu, hya, hyb)
    part, _, xu, _, _ = pl.pallas_call(
        lambda *refs: outer_kernel(batch, *refs),
        out_shape=(shape((3 * count // 4, 2 * count), F32), fields, both, fields, fields),
        in_specs=[vmem] * 12,
        out_specs=(vmem,) * 5,
        scratch_shapes=[halo, halo],
        input_output_aliases={0: 1, 1: 2, 2: 3, 3: 4},
        compiler_params=params,
        name="rim",
    )(e0, xu, e1, e2, hxa, hxb, hya, hyb, ca, cb, acc, s_gram)
    total = total_sum(part)
    cells = float(cols * width * lax.axis_size("gx") * lax.axis_size("gy"))
    basis, core = pl.pallas_call(
        lambda *refs: last_kernel(batch, cells, *refs),
        out_shape=(shape(snapshots.shape, F32), shape((count + batch, count + batch), F32)),
        in_specs=[vmem] * 3,
        out_specs=(hbm, vmem),
        scratch_shapes=[pltpu.VMEM((cols, batch, width), F32), pltpu.SemaphoreType.DMA((cols,))],
        compiler_params=params,
        name="last",
    )(total, sigma.reshape(1, count), xu)
    return (basis, core)


def solution(mesh):
    return jax.shard_map(
        body,
        mesh=mesh,
        in_specs=(
            P(None, "gx", "gy"),
            P(None, "gx", "gy"),
            P("gx", "gy"),
            P("gx", "gy"),
            P("gx", "gy"),
            P(),
        ),
        out_specs=(P(None, "gx", "gy"), P()),
        check_vma=False,
    )
```

```python
import jax
import jax.numpy as jnp
from jax import lax
from jax.experimental import pallas as pl
from jax.experimental.pallas import tpu as pltpu
from jax.sharding import PartitionSpec as P

NZ = 24
STEPS = 3
LANES = 128
ROWS = 32
UNROLL = 7
GROUP = 8
HIGH = lax.Precision.HIGHEST
F32 = jnp.float32
BF16 = jnp.bfloat16


def split(value):
    high = value.astype(BF16)
    return high, (value - high.astype(F32)).astype(BF16)


def dot_t(a, b):
    return lax.dot_general(a, b, (((1,), (1,)), ((), ())), preferred_element_type=F32)


def small_dot(a, b, dims=((1,), (0,))):
    return lax.dot_general(a, b, (dims, ((), ())), precision=HIGH, preferred_element_type=F32)


def fill_rows(dst, index, fields, rate, keep):
    batch = fields.shape[0]
    dst[index + (pl.ds(0, batch),)] = fields
    dst[index + (pl.ds(batch, 1),)] = rate
    dst[index + (pl.ds(batch + 1, 1),)] = keep
    dst[index + (pl.ds(batch + 2, ROWS - batch - 2),)] = jnp.zeros((ROWS - batch - 2, LANES), F32)


def pack_spots(cols):
    span = STEPS * NZ
    return [(r, r * span // LANES, r * span % LANES) for r in range(cols)]


def packed_tiles(cols):
    return pl.cdiv(cols * STEPS * NZ, LANES)


def edge_kernel(snap, mob, pha, con, coef, sxa, sxb, sya, syb, bufx, bufy, vm, vp, vc, rows, cols_y, packed, sem, sem_c):
    batch, cols, width = snap.shape
    tiles = width // LANES
    small = [
        pltpu.make_async_copy(ref, dst, sem_c.at[i])
        for i, (ref, dst) in enumerate(((mob, vm), (pha, vp), (con, vc)))
    ]
    outer = list(range(STEPS)) + list(range(cols - STEPS, cols))
    inner = list(range(STEPS, cols - STEPS))
    copies = [pltpu.make_async_copy(snap.at[:, i, :], bufx.at[k], sem.at[k]) for k, i in enumerate(outer)]
    for k, i in enumerate(inner):
        for side, start in enumerate((0, width - LANES)):
            n = len(outer) + 2 * k + side
            copies.append(
                pltpu.make_async_copy(snap.at[:, i, pl.ds(start, LANES)], bufy.at[k, side], sem.at[n])
            )
    for copy in small + copies:
        copy.start()
    for copy in small:
        copy.wait()
    rate = vm[...] * jnp.where(vp[...] == 1, 1.0, 0.5).astype(F32)
    lane = lax.broadcasted_iota(jnp.int32, (cols, width), 1) % NZ
    ends = jnp.where(lane == 0, 1.0, 0.0) + jnp.where(lane == NZ - 1, 1.0, 0.0)
    keep = 1.0 - 0.25 * vc[...].astype(F32) - rate * (6.0 - ends)
    coef[0] = rate
    coef[1] = keep
    for k, i in enumerate(outer):
        copies[k].wait()
        for t in range(tiles):
            span = slice(t * LANES, (t + 1) * LANES)
            fill_rows(rows, (k, t), bufx[k, :, span], rate[i : i + 1, span], keep[i : i + 1, span])
        for side, t in enumerate((0, tiles - 1)):
            cols_y[side, i] = rows[k, t]
    for k, i in enumerate(inner):
        for side, t in enumerate((0, tiles - 1)):
            copies[len(outer) + 2 * k + side].wait()
            span = slice(t * LANES, (t + 1) * LANES)
            fill_rows(cols_y, (side, i), bufy[k, side], rate[i : i + 1, span], keep[i : i + 1, span])
    odd_x = lax.rem(lax.axis_index("gx"), 2)
    odd_y = lax.rem(lax.axis_index("gy"), 2)
    sxa[...] = rows[pl.ds((1 - odd_x) * STEPS, STEPS)]
    sxb[...] = rows[pl.ds(odd_x * STEPS, STEPS)]
    wide = lax.broadcasted_iota(jnp.int32, (ROWS, LANES), 1)
    span = STEPS * NZ
    for side in range(2):
        tail = None
        for r, tile, spot in pack_spots(cols):
            value = pltpu.roll(cols_y[side, r], (spot + side * span) % LANES, 1)
            packed[side, tile] = value if spot == 0 else jnp.where(wide >= spot, value, tail)
            if spot + span < LANES:
                tail = packed[side, tile]
            else:
                tail = value
                if tile + 1 < packed.shape[1]:
                    packed[side, tile + 1] = value
    sya[...] = packed[1 - odd_y]
    syb[...] = packed[odd_y]


def modes_kernel(modes, snap, coef, xu, gram, e0, buf, bufx, sem):
    count, cols, width = modes.shape
    batch = snap.shape[0]
    tiles = width // LANES
    copies = [
        pltpu.make_async_copy(source.at[:, :, pl.ds(t * LANES, LANES)], target.at[t], sem.at[k * tiles + t])
        for k, (source, target) in enumerate(((snap, bufx), (modes, buf)))
        for t in range(tiles)
    ]
    for copy in copies:
        copy.start()
    empty = jnp.zeros((ROWS - batch - 2, 8, LANES), F32)
    for t in range(tiles):
        copies[t].wait()
        lanes = slice(t * LANES, (t + 1) * LANES)
        for start in range(0, cols, 8):
            part = slice(start, start + 8)
            block = [bufx[t, :, part, :], coef[0, part, lanes][None], coef[1, part, lanes][None], empty]
            block = jnp.swapaxes(jnp.concatenate(block, 0), 0, 1)
            for i in range(8):
                e0[STEPS + start + i, t] = block[i]
    for t in range(tiles):
        copies[tiles + t].wait()
        lanes = slice(t * LANES, (t + 1) * LANES)
        for start in range(0, cols, 8):
            block = jnp.swapaxes(buf[t, :, start : start + 8, :], 0, 1)
            for i in range(8):
                high, low = split(block[i])
                xu[start + i, 0:count, lanes] = high
                xu[start + i, count : 2 * count, lanes] = low
    acc = None
    for i in range(cols):
        part = dot_t(xu[i, 0 : 2 * count, :], xu[i, 0:count, :])
        acc = part if acc is None else acc + part
    cross = acc[count : 2 * count]
    gram[...] = acc[0:count] + (cross + cross.T)


def z_masks(tiles):
    lane = lax.broadcasted_iota(jnp.int32, (8, LANES), 1)
    found = []
    for t in range(tiles + 1):
        z = (lane + t * LANES) % NZ if t < tiles else jnp.where(lane < LANES // 2, lane % NZ, (lane + 16) % NZ)
        found.append((jnp.where(z == 0, 0.0, 1.0), jnp.where(z == NZ - 1, 0.0, 1.0)))
    return found


def row_coef(base, row, batch, tiles):
    return [
        [jnp.broadcast_to(base[row, t, pl.ds(batch + k, 1), :], (8, LANES)) for k in range(2)] for t in range(tiles)
    ]


def step_row(src, coef, row, group, masks, ring, last):
    tiles = len(masks) - 1
    s = pl.ds(group * 8, 8)
    lane = lax.broadcasted_iota(jnp.int32, (8, LANES), 1)
    here = [src[row, t, s, :] for t in range(tiles + 1)]
    if ring is None:
        low, high = here[tiles], here[tiles]
    else:
        low, high = ring[0][row - 1, s, :], ring[1][row - 1, s, :]
    fwd = [pltpu.roll(h, NZ, 1) for h in here[:tiles] + [low]]
    bwd = [pltpu.roll(h, LANES - NZ, 1) for h in here[:tiles] + [high]]
    own = (fwd[tiles], bwd[tiles])
    if ring is not None:
        half = lane < LANES // 2
        own = (
            jnp.where(half, pltpu.roll(high, NZ, 1), fwd[tiles]),
            jnp.where(half, bwd[tiles], pltpu.roll(low, LANES - NZ, 1)),
        )
    one = [pltpu.roll(h, 1, 1) for h in here]
    neg = [pltpu.roll(h, LANES - 1, 1) for h in here]
    new = []
    for t in range(tiles if last else tiles + 1):
        before, after = (t - 1) % (tiles + 1), (t + 1) % (tiles + 1)
        mine = own if t == tiles else (fwd[t], bwd[t])
        beside = (src[row - 1, t, s, :] + src[row + 1, t, s, :]) + (
            jnp.where(lane < NZ, fwd[before], mine[0]) + jnp.where(lane >= LANES - NZ, bwd[after], mine[1])
        )
        starts = (t * LANES) % NZ == 0
        stops = ((t + 1) * LANES) % NZ == 0
        below = one[t] if starts else jnp.where(lane < 1, one[before], one[t])
        above = neg[t] if stops else jnp.where(lane >= LANES - 1, neg[after], neg[t])
        beside = beside + (masks[t][0] * below + masks[t][1] * above)
        new.append(coef[t][1] * here[t] + coef[t][0] * beside)
    return new


def place_sides(e0, low, high, sides, ends, rows):
    cols = e0.shape[0] - 2 * STEPS
    tiles = e0.shape[1] - 1
    span = STEPS * NZ
    spots = pack_spots(cols)
    lane = lax.broadcasted_iota(jnp.int32, (ROWS, LANES), 1)

    def place(lo, hi, lo_ends, hi_ends):
        for r in rows:
            k = r - 2
            if 0 <= k < cols:
                _, tile, spot = spots[k]
                lo_row, hi_row = lo[tile], hi[tile]
                if spot + span > LANES:
                    lo_row = jnp.where(lane >= spot, lo_row, lo[tile + 1])
                    hi_row = jnp.where(lane >= spot, hi_row, hi[tile + 1])
                lo_row = pltpu.roll(lo_row, (2 * LANES - span - spot) % LANES, 1)
                hi_row = pltpu.roll(hi_row, (LANES - spot) % LANES, 1)
            else:
                end = r if k < 0 else r - cols
                lo_row, hi_row = lo_ends[end], hi_ends[end]
            low[r] = lo_row
            high[r] = hi_row
            e0[r + 1, tiles] = jnp.where(lane < LANES // 2, hi_row, lo_row)

    odd_y = lax.rem(lax.axis_index("gy"), 2) == 1
    pl.when(odd_y)(lambda: place(sides[0], sides[1], ends[0], ends[1]))
    pl.when(jnp.logical_not(odd_y))(lambda: place(sides[1], sides[0], ends[1], ends[0]))


def sweep(src, dst, base, start, stop, batch, masks, ring):
    tiles = len(masks)
    unroll = max(u for u in range(1, UNROLL + 1) if (stop - start) % u == 0)

    @pl.loop(0, (stop - start) // unroll)
    def _(k):
        for j in range(unroll):
            row = start + k * unroll + j
            coef = row_coef(base, row, batch, tiles)
            for group in range(ROWS // 8):
                for t, v in enumerate(step_row(src, coef, row, group, masks, ring, False)):
                    dst[row, t, pl.ds(group * 8, 8), :] = v


def final_sweep(src, xu, base, start, stop, batch, masks):
    tiles = len(masks) - 1
    first = xu.shape[1] - 2 * ROWS
    unroll = max(u for u in range(1, UNROLL + 1) if (stop - start) % u == 0)

    @pl.loop(0, (stop - start) // unroll)
    def _(k):
        for j in range(unroll):
            i = start + k * unroll + j
            coef = row_coef(base, i + STEPS, batch, tiles)
            for pair in range(ROWS // 16):
                parts = [step_row(src, coef, i + STEPS, 2 * pair + h, masks, None, True) for h in range(2)]
                for t in range(tiles):
                    h, l = split(jnp.concatenate([parts[0][t], parts[1][t]], 0))
                    xu[i, pl.ds(first + pair * 16, 16), t * LANES : (t + 1) * LANES] = h
                    xu[i, pl.ds(first + ROWS + pair * 16, 16), t * LANES : (t + 1) * LANES] = l


def products(xu, rows, acc):
    first = xu.shape[1] - 2 * ROWS
    for i in rows:
        part = dot_t(xu[i], xu[i, first:, :])
        acc = part if acc is None else acc + part
    return acc


def inner_kernel(batch, e0_in, xu_in, hya, hyb, acc, e0, xu, e1, e2, low, high):
    cols = xu.shape[0]
    masks = z_masks(e0.shape[1] - 1)
    place_sides(e0, low, high, (hya, hyb), (None, None), range(2, cols + 2))
    sweep(e0, e1, e0, STEPS + 1, cols + STEPS - 1, batch, masks, (low, high))
    sweep(e1, e2, e0, STEPS + 2, cols + STEPS - 2, batch, masks, None)
    final_sweep(e2, xu, e0, STEPS, cols - STEPS, batch, masks)
    acc[...] = products(xu, range(STEPS, cols - STEPS), None)


def outer_kernel(batch, e0_in, xu_in, e1_in, e2_in, hxa, hxb, hya, hyb, ca, cb, acc_in, s_gram, out, e0, xu, e1, e2, low, high):
    cols = xu.shape[0]
    tiles = e0.shape[1] - 1
    base = xu.shape[1] - 2 * ROWS
    count = base // 2
    odd_x = lax.rem(lax.axis_index("gx"), 2) == 1
    e0[0, tiles] = jnp.zeros((ROWS, LANES), F32)
    e0[cols + 2 * STEPS - 1, tiles] = jnp.zeros((ROWS, LANES), F32)

    def place_x(up, down):
        e0[0:STEPS, 0:tiles] = up[...]
        e0[cols + STEPS :, 0:tiles] = down[...]

    pl.when(odd_x)(lambda: place_x(hxa, hxb))
    pl.when(jnp.logical_not(odd_x))(lambda: place_x(hxb, hxa))
    place_sides(e0, low, high, (hya, hyb), (ca, cb), (0, 1, 2, cols + 1, cols + 2, cols + 3))
    masks = z_masks(tiles)
    sweep(e0, e1, e0, 1, STEPS + 1, batch, masks, (low, high))
    sweep(e0, e1, e0, cols + STEPS - 1, cols + 5, batch, masks, (low, high))
    sweep(e1, e2, e0, 2, STEPS + 2, batch, masks, None)
    sweep(e1, e2, e0, cols + STEPS - 2, cols + 4, batch, masks, None)
    final_sweep(e2, xu, e0, 0, STEPS, batch, masks)
    final_sweep(e2, xu, e0, cols - STEPS, cols, batch, masks)
    acc = products(xu, list(range(STEPS)) + list(range(cols - STEPS, cols)), acc_in[...])
    u = acc[0:count, :] + acc[count:base, :]
    x = acc[base : base + ROWS, :] + acc[base + ROWS :, :]
    u = u[:, 0:ROWS] + u[:, ROWS:]
    s = s_gram[...]
    half = count // 2
    quarter = half // 2
    x = x[:, 0:ROWS] + x[:, ROWS:]
    out[0:half, :] = jnp.concatenate([u[0:half], u[half:], x, s[0:half, half:]], 1)
    corner = [s[k * half : (k + 1) * half, k * half : (k + 1) * half] for k in range(2)]
    out[half:, :] = jnp.concatenate([c[k * quarter : (k + 1) * quarter] for c in corner for k in range(2)], 1)


def last_kernel(batch, cells, total, sigma, xu, basis, core, buf, sem):
    cols = xu.shape[0]
    count = xu.shape[1] // 2 - ROWS
    half = count // 2
    inverse = 1.0 / cells
    blocks = [total[0:half, k * half : (k + 1) * half] for k in range(4)]
    pieces = [total[half:, k * half : (k + 1) * half] for k in range(4)]
    col = lax.broadcasted_iota(jnp.int32, (count, ROWS), 1)
    c = jnp.where(col < batch, jnp.concatenate(blocks[:2], 0), 0.0)
    rows = lax.broadcasted_iota(jnp.int32, (ROWS, ROWS), 0)
    lanes = lax.broadcasted_iota(jnp.int32, (ROWS, ROWS), 1)
    g = blocks[2]
    s = jnp.concatenate(
        [
            jnp.concatenate([jnp.concatenate(pieces[:2], 0), blocks[3]], 1),
            jnp.concatenate([blocks[3].T, jnp.concatenate(pieces[2:], 0)], 1),
        ],
        0,
    )
    first = c * inverse
    both = first + (c - small_dot(s, first)) * inverse
    rest = small_dot(s, both) - c
    gram = g - small_dot(c, both, ((0,), (0,))) + small_dot(both, rest, ((0,), (0,)))
    gram = jnp.where((rows < batch) & (lanes < batch), gram * inverse, jnp.where(rows == lanes, 1.0, 0.0))
    m = jnp.concatenate([gram, jnp.where(rows == lanes, 1.0, 0.0)], 1)
    index = lax.broadcasted_iota(jnp.int32, (8, LANES), 0)
    groups = ROWS // 8
    m = jnp.concatenate([m, jnp.zeros((ROWS, LANES - 2 * ROWS), F32)], 1)
    m = [m[8 * q : 8 * q + 8] for q in range(groups)]
    columns = [[jnp.broadcast_to(m[q][:, j : j + 1], (8, LANES)) for q in range(groups)] for j in range(batch)]
    for j in range(batch):
        at, row = j // 8, j % 8
        pivot = columns[j][at][row : row + 1]
        factor = {}
        for q in range(at, groups):
            value = columns[j][q] * (1.0 / pivot)
            factor[q] = jnp.where(index > row, value, 0.0) if q == at else value
        for k in range(j + 1, batch):
            top = columns[k][at][row : row + 1]
            for q in range(at, groups):
                columns[k][q] = columns[k][q] - factor[q] * top
        top = m[at][row : row + 1]
        for q in range(at, groups):
            m[q] = m[q] - factor[q] * top
        m[at] = jnp.where(index == row, m[at] * lax.rsqrt(pivot), m[at])
    m = jnp.concatenate(m, 0)
    upper = jnp.where(rows <= lanes, m[:, 0:ROWS], 0.0)
    linv = m[:, ROWS : 2 * ROWS]
    wu = -small_dot(linv, both, ((1,), (1,)))
    xh, xl = split(linv)
    uh, ul = split(wu)
    w = jnp.concatenate(
        [jnp.concatenate([uh, uh, xh, xh], 1), jnp.concatenate([ul, ul, xl, xl], 1)], 0
    )
    copies = [pltpu.make_async_copy(buf.at[i], basis.at[:, i, :], sem.at[i]) for i in range(cols)]
    for start in range(0, cols, GROUP):
        for i in range(start, start + GROUP):
            value = jnp.dot(w, xu[i], preferred_element_type=F32)
            buf[i] = value[0:batch] + value[ROWS : ROWS + batch]
        for i in range(start, start + GROUP):
            copies[i].start()
    core[...] = jnp.zeros_like(core)
    er = lax.broadcasted_iota(jnp.int32, (count, count), 0)
    ec = lax.broadcasted_iota(jnp.int32, (count, count), 1)
    core[0:count, 0:count] = jnp.where(er == ec, sigma[...], 0.0)
    core[0:count, count:] = both[:, 0:batch]
    core[count:, count:] = upper[0:batch, 0:batch]
    for copy in copies:
        copy.wait()


def in_hbm(value):
    return pltpu.with_memory_space_constraint(value, pltpu.HBM)


def swap(value, axis, offset):
    count = lax.axis_size(axis)
    pairs = [(i, i + 1) for i in range(offset, count - 1, 2)]
    return lax.ppermute(value, axis, pairs + [(j, i) for i, j in pairs])


def exchanged_sum(value, axis, offsets):
    count = lax.axis_size(axis)
    terms = [value] + [lax.ppermute(value, axis, [(i, i ^ k) for i in range(count)]) for k in offsets]
    while len(terms) > 1:
        terms = [a + b for a, b in zip(terms[::2], terms[1::2])]
    return terms[0]


def total_sum(value):
    for axis in ("gy", "gx"):
        count = lax.axis_size(axis)
        if count & (count - 1):
            value = lax.psum(value, axis)
            continue
        step = 1
        while step < count:
            odd = (count // step).bit_length() % 2 == 0
            value = exchanged_sum(value, axis, [step] if odd else [step, 2 * step, 3 * step])
            step *= 2 if odd else 4
    return value


def body(snapshots, modes, mobility, phase, contact, sigma):
    batch, cols, width = snapshots.shape
    count = modes.shape[0]
    tiles = width // LANES
    vmem = pl.BlockSpec(memory_space=pltpu.VMEM)
    hbm = pl.BlockSpec(memory_space=pltpu.HBM)
    shape = jax.ShapeDtypeStruct
    params = pltpu.CompilerParams(vmem_limit_bytes=40 << 20)
    coef, sxa, sxb, sya, syb = pl.pallas_call(
        edge_kernel,
        out_shape=(shape((2, cols, width), F32),)
        + (shape((STEPS, tiles, ROWS, LANES), F32),) * 2
        + (shape((packed_tiles(cols), ROWS, LANES), F32),) * 2,
        in_specs=[hbm] * 4,
        out_specs=(vmem,) * 5,
        scratch_shapes=[
            pltpu.VMEM((2 * STEPS, batch, width), F32),
            pltpu.VMEM((cols - 2 * STEPS, 2, batch, LANES), F32),
            pltpu.VMEM((cols, width), F32),
            pltpu.VMEM((cols, width), jnp.int32),
            pltpu.VMEM((cols, width), jnp.int32),
            pltpu.VMEM((2 * STEPS, tiles, ROWS, LANES), F32),
            pltpu.VMEM((2, cols, ROWS, LANES), F32),
            pltpu.VMEM((2, packed_tiles(cols), ROWS, LANES), F32),
            pltpu.SemaphoreType.DMA((2 * cols - 2 * STEPS,)),
            pltpu.SemaphoreType.DMA((3,)),
        ],
        compiler_params=params,
        name="edge",
    )(*(in_hbm(v) for v in (snapshots, mobility, phase, contact)))
    odd_x = lax.axis_index("gx") % 2 == 1
    odd_y = lax.axis_index("gy") % 2 == 1
    hxa = swap(sxa, "gx", 0)
    hxb = swap(sxb, "gx", 1)
    hya = swap(sya, "gy", 0)
    hyb = swap(syb, "gy", 1)
    ext = (cols + 2 * STEPS, tiles + 1, ROWS, LANES)
    xu, s_gram, e0 = pl.pallas_call(
        modes_kernel,
        out_shape=(shape((cols, 2 * (count + ROWS), width), BF16), shape((count, count), F32), shape(ext, F32)),
        in_specs=[hbm, hbm, vmem],
        out_specs=(vmem,) * 3,
        scratch_shapes=[
            pltpu.VMEM((tiles, count, cols, LANES), F32),
            pltpu.VMEM((tiles, batch, cols, LANES), F32),
            pltpu.SemaphoreType.DMA((2 * tiles,)),
        ],
        compiler_params=params,
        cost_estimate=pl.CostEstimate(flops=2 * cols * width * 4 * count * count, bytes_accessed=8 * cols * width * count, transcendentals=0),
        name="modes",
    )(in_hbm(modes), in_hbm(snapshots), coef)
    hxa, hxb, s_gram = lax.optimization_barrier((hxa, hxb, s_gram))

    def corners(low_side):
        side = [jnp.where(low_side, h[:, 0], h[:, tiles - 1]) for h in (hxa, hxb)]
        up = jnp.where(odd_x, side[0][1:], side[1][1:])
        down = jnp.where(odd_x, side[1][:2], side[0][:2])
        return jnp.concatenate([up, down], 0)

    ca = swap(corners(odd_y), "gy", 0)
    cb = swap(corners(jnp.logical_not(odd_y)), "gy", 1)
    halo = pltpu.VMEM((cols + 4, ROWS, LANES), F32)
    fields = shape(ext, F32)
    both = shape((cols, 2 * (count + ROWS), width), BF16)
    acc, e0, xu, e1, e2 = pl.pallas_call(
        lambda *refs: inner_kernel(batch, *refs),
        out_shape=(shape((2 * (count + ROWS), 2 * ROWS), F32), fields, both, fields, fields),
        in_specs=[vmem] * 4,
        out_specs=(vmem,) * 5,
        scratch_shapes=[halo, halo],
        input_output_aliases={0: 1, 1: 2},
        compiler_params=params,
        cost_estimate=pl.CostEstimate(flops=40 * cols * width * ROWS, bytes_accessed=8 * cols * width * count, transcendentals=0),
        name="inner",
    )(e0, xu, hya, hyb)
    part, _, xu, _, _ = pl.pallas_call(
        lambda *refs: outer_kernel(batch, *refs),
        out_shape=(shape((3 * count // 4, 2 * count), F32), fields, both, fields, fields),
        in_specs=[vmem] * 12,
        out_specs=(vmem,) * 5,
        scratch_shapes=[halo, halo],
        input_output_aliases={0: 1, 1: 2, 2: 3, 3: 4},
        compiler_params=params,
        name="rim",
    )(e0, xu, e1, e2, hxa, hxb, hya, hyb, ca, cb, acc, s_gram)
    total = total_sum(part)
    cells = float(cols * width * lax.axis_size("gx") * lax.axis_size("gy"))
    basis, core = pl.pallas_call(
        lambda *refs: last_kernel(batch, cells, *refs),
        out_shape=(shape(snapshots.shape, F32), shape((count + batch, count + batch), F32)),
        in_specs=[vmem] * 3,
        out_specs=(hbm, vmem),
        scratch_shapes=[pltpu.VMEM((cols, batch, width), F32), pltpu.SemaphoreType.DMA((cols,))],
        compiler_params=params,
        name="last",
    )(total, sigma.reshape(1, count), xu)
    return (basis, core)


def solution(mesh):
    return jax.shard_map(
        body,
        mesh=mesh,
        in_specs=(
            P(None, "gx", "gy"),
            P(None, "gx", "gy"),
            P("gx", "gy"),
            P("gx", "gy"),
            P("gx", "gy"),
            P(),
        ),
        out_specs=(P(None, "gx", "gy"), P()),
        check_vma=False,
    )
```
